256 devices in a mesh: seq: 32 (over y, z_lo, core), kvh: 8 (over x, z_hi).
Axes of the slice: x: 4, y: 4, z: 8 (z_hi: 2, z_lo: 4; z = z_hi * 4 + z_lo), core: 2. Of those that a mesh axis runs over, the one named last changes fastest.
Arguments:
- queries: bfloat16 [8192, 8192], P('seq', 'kvh'), may hold values from -2.5 to 2.5
- key_vector_rows: bfloat16 [8192, 1024], P(('seq', 'kvh')), may hold values from -2.5 to 2.5
- value_vector_rows: bfloat16 [8192, 1024], P(('seq', 'kvh')), may hold values from -5 to 5
- output_gradient: bfloat16 [8192, 8192], P('seq', 'kvh'), may hold values from -24 to 24
- key_lists: int32 [64, 24], replicated, may hold values from 0 to 63, as said below
- block_counts: int32 [64], replicated, may hold values from 1 to 24, as said below
- span_table: int32 [64], replicated, may hold values from 0 to 63, each once
Outputs:
- grad_queries: bfloat16 [8192, 8192], P('seq', 'kvh')
- key_gradient: bfloat16 [8192, 1024], P(('seq', 'kvh'))
- value_gradient: bfloat16 [8192, 1024], P(('seq', 'kvh'))
The draws below stay inside these ranges and needn't reach their ends.
Inputs may be any that keep to these rules, and one draw needn't show every extreme that they name: `key_lists`: row b lists, by position, the key blocks of query block b: its first block_counts[b] entries are distinct blocks at or before b, the first being b itself; the remaining entries are 0. block_counts[b] is at most b + 1 and at most 24; the last block's count is 24. `span_table`: each position block appears once.
All inputs are finite; a program needn't handle non-finite values.
Results may differ from the reference program's by a relative error of at most 0.0055.
Values may be sent and summed in bfloat16 or wider, within the bound.
A program may use at most 128 MiB of HBM per device.

```python
import jax
import jax.numpy as jnp
from jax import lax

HEAD_SIZE = 128
QUERY_PER_KEY = 8
BLOCK_TOKENS = 128
NB = 24
BLOCK_COUNT = 64
TRAJECTORY_LEN = 8192
KEY_VALUE_HEADS = 8
HQ = 64


def lists_and_counts(key):
    base_key = jax.random.fold_in(key, 11)
    first_key, second_key = jax.random.split(base_key)
    block_ids = jnp.arange(BLOCK_COUNT, dtype=jnp.int32)
    limits = jax.random.randint(first_key, (BLOCK_COUNT,), (NB + 1) // 2, NB + 1, dtype=jnp.int32)
    limits = jnp.where(block_ids == BLOCK_COUNT - 1, NB, limits)
    counts_drawn = jnp.minimum(block_ids + 1, limits).astype(jnp.int32)
    columns = block_ids[None, :]
    random_rank = jax.random.randint(second_key, (BLOCK_COUNT, BLOCK_COUNT), 0, 1 << 20, dtype=jnp.int32)
    eligible = jnp.logical_and(columns >= 1, columns <= block_ids[:, None] - 2)
    ranked = jnp.where(eligible, random_rank * BLOCK_COUNT + columns, (1 << 30) + columns)
    chosen = lax.top_k(-ranked, NB)[1].astype(jnp.int32)
    fixed_part = jnp.stack([block_ids, block_ids - 1, jnp.zeros_like(block_ids)], 1)
    lists = jnp.concatenate([fixed_part, chosen[:, :NB - 3]], 1)
    entry_ids = jnp.arange(NB, dtype=jnp.int32)[None, :]
    lists = jnp.where(entry_ids < counts_drawn[:, None], lists, 0).astype(jnp.int32)
    return (lists, counts_drawn)


def draw_key_lists(key, part):
    return lists_and_counts(key)[0]


def draw_block_counts(key, part):
    return lists_and_counts(key)[1]


def shard_levels(stream_key, dims, shards, low, top_value):
    factor_of = 1.0
    for axis_at, shards_of in shards:
        heights = jax.random.uniform(jax.random.fold_in(jax.random.fold_in(stream_key, 6), axis_at), (shards_of,), jnp.float32, low / len(shards), top_value / len(shards))
        factor_of = factor_of * jnp.repeat(jnp.exp(heights), dims[axis_at] // shards_of).reshape((-1,) + (1,) * (len(dims) - 1 - axis_at))
    return factor_of


def normal_values(own_key, shape, spread, bound, cuts=(), held_as=jnp.bfloat16):
    result = spread * jax.random.normal(own_key, shape, jnp.float32)
    if cuts:
        result = result * shard_levels(own_key, shape, cuts, -0.22, 0.18)
    return jnp.clip(result, -bound, bound).astype(held_as)


def setup_inputs(seed: int = 0) -> dict:
    key_list = jax.random.split(jax.random.key(seed), 8)
    queries = normal_values(key_list[0], (TRAJECTORY_LEN, HQ * HEAD_SIZE), 1.0, 2.5, ((0, 32), (1, 8)))
    key_vector_rows = normal_values(key_list[1], (TRAJECTORY_LEN, KEY_VALUE_HEADS * HEAD_SIZE), 1.0, 2.5, ((0, 256),))
    value_vector_rows = normal_values(key_list[2], (TRAJECTORY_LEN, KEY_VALUE_HEADS * HEAD_SIZE), 1.0, 5.0, ((0, 256),))
    output_gradient = normal_values(key_list[3], (TRAJECTORY_LEN, HQ * HEAD_SIZE), 4.0, 24.0, ((0, 32), (1, 8)))
    key_lists = draw_key_lists(jax.random.fold_in(key_list[7], 71), 0)
    block_counts = draw_block_counts(jax.random.fold_in(key_list[7], 71), 0)
    span_table = jax.random.permutation(key_list[6], BLOCK_COUNT).astype(jnp.int32)
    return {"queries": queries, "key_vector_rows": key_vector_rows, "value_vector_rows": value_vector_rows, "output_gradient": output_gradient, "key_lists": key_lists, "block_counts": block_counts, "span_table": span_table}


def rounded(values_in):
    return lax.optimization_barrier(values_in.astype(jnp.bfloat16)).astype(jnp.float32)


def reference(queries, key_vector_rows, value_vector_rows, output_gradient, key_lists, block_counts, span_table):
    logit_scale = HEAD_SIZE ** -0.5
    blocked_queries = queries.astype(jnp.float32).reshape(BLOCK_COUNT, BLOCK_TOKENS, KEY_VALUE_HEADS, QUERY_PER_KEY, HEAD_SIZE)
    blocked_keys = key_vector_rows.astype(jnp.float32).reshape(BLOCK_COUNT, BLOCK_TOKENS, KEY_VALUE_HEADS, HEAD_SIZE)
    blocked_values = value_vector_rows.astype(jnp.float32).reshape(BLOCK_COUNT, BLOCK_TOKENS, KEY_VALUE_HEADS, HEAD_SIZE)
    gradient_block_list = output_gradient.astype(jnp.float32).reshape(BLOCK_COUNT, BLOCK_TOKENS, KEY_VALUE_HEADS, QUERY_PER_KEY, HEAD_SIZE)
    block_ids = jnp.arange(BLOCK_COUNT, dtype=jnp.int32)
    inverse = jnp.zeros((BLOCK_COUNT,), jnp.int32).at[span_table].set(block_ids)
    lower_mask = jnp.arange(BLOCK_TOKENS)[None, :] <= jnp.arange(BLOCK_TOKENS)[:, None]

    def slot_step(carried, slot):
        key_gradient_total, value_gradient_total = carried
        query_pos = span_table[slot]
        entries = block_counts[query_pos]
        query_blk = blocked_queries[slot]
        grad_blk = gradient_block_list[slot]

        def scored(entry_id):
            key_pos = key_lists[query_pos, entry_id]
            key_slot = inverse[key_pos]
            key_blk = blocked_keys[key_slot]
            value_blk = blocked_values[key_slot]
            scores = jnp.einsum("thgd,shd->hgts", query_blk, key_blk) * logit_scale
            allowed = jnp.logical_or(key_pos != query_pos, lower_mask)
            return scores, allowed, key_blk, value_blk, key_slot

        def forward_step(entry_id, state_pair):
            row_total, weighted = state_pair
            scores, allowed, key_blk, value_blk, key_slot = scored(entry_id)
            exp_scores = jnp.where(allowed, jnp.exp(scores), jnp.float32(0.0))
            row_total = row_total + jnp.sum(exp_scores, -1)
            weighted = weighted + jnp.einsum("hgts,shd->thgd", rounded(exp_scores), value_blk)
            return row_total, weighted

        starting_carry = (jnp.zeros((KEY_VALUE_HEADS, QUERY_PER_KEY, BLOCK_TOKENS), jnp.float32), jnp.zeros((BLOCK_TOKENS, KEY_VALUE_HEADS, QUERY_PER_KEY, HEAD_SIZE), jnp.float32))
        row_total, weighted = lax.fori_loop(0, entries, forward_step, starting_carry)
        log_total = jnp.log(row_total)
        attended = weighted / jnp.transpose(row_total, (2, 0, 1))[..., None]
        row_delta = jnp.transpose(jnp.sum(grad_blk * attended, -1), (1, 2, 0))

        def backward_step(entry_id, state_triple):
            query_grad, key_inner, value_inner = state_triple
            scores, allowed, key_blk, value_blk, key_slot = scored(entry_id)
            weights = jnp.where(allowed, jnp.exp(scores - log_total[..., None]), jnp.float32(0.0))
            value_part = jnp.einsum("hgts,thgd->shd", rounded(weights), grad_blk)
            weight_grads = jnp.einsum("thgd,shd->hgts", grad_blk, value_blk)
            score_grads = rounded(weights * (weight_grads - row_delta[..., None]))
            query_grad = query_grad + jnp.einsum("hgts,shd->thgd", score_grads, key_blk)
            key_part = jnp.einsum("hgts,thgd->shd", score_grads, query_blk)
            key_inner = key_inner.at[key_slot].add(key_part)
            value_inner = value_inner.at[key_slot].add(value_part)
            return query_grad, key_inner, value_inner

        initial_gradient = jnp.zeros((BLOCK_TOKENS, KEY_VALUE_HEADS, QUERY_PER_KEY, HEAD_SIZE), jnp.float32)
        query_grad, key_gradient_total, value_gradient_total = lax.fori_loop(0, entries, backward_step, (initial_gradient, key_gradient_total, value_gradient_total))
        return (key_gradient_total, value_gradient_total), (query_grad * logit_scale).astype(jnp.bfloat16)

    empty_totals = jnp.zeros((BLOCK_COUNT, BLOCK_TOKENS, KEY_VALUE_HEADS, HEAD_SIZE), jnp.float32)
    (key_gradient_total, value_gradient_total), query_out = lax.scan(slot_step, (empty_totals, empty_totals), block_ids)
    grad_queries = query_out.reshape(TRAJECTORY_LEN, HQ * HEAD_SIZE)
    key_gradient = (key_gradient_total * logit_scale).astype(jnp.bfloat16).reshape(TRAJECTORY_LEN, KEY_VALUE_HEADS * HEAD_SIZE)
    value_gradient = value_gradient_total.astype(jnp.bfloat16).reshape(TRAJECTORY_LEN, KEY_VALUE_HEADS * HEAD_SIZE)
    return (grad_queries, key_gradient, value_gradient)
```

```python
import jax
import jax.numpy as jnp
from jax import lax
from jax.experimental import pallas as pl
from jax.experimental.pallas import tpu as pltpu
from jax.sharding import PartitionSpec as P
H = 128
G = 8
B = 128
NB = 24
NBLK = 64
SC = H ** -0.5
C2 = SC * 1.4426950408889634
R = G * B
bf = jnp.bfloat16
f32 = jnp.float32


def attn_kernel(slots, counts, inv, q_ref, do_ref, kv_ref, dq_ref, part,
                qT, doT, qr, dor, e_buf, p_buf, dkb, dvb, dqT):
    dkb[2 * NB] = jnp.zeros((B, H), f32)
    dvb[2 * NB] = jnp.zeros((B, H), f32)
    for j in range(2):
        for g in range(G):
            qb = q_ref[j * B:(j + 1) * B, g * H:(g + 1) * H]
            ob = do_ref[j * B:(j + 1) * B, g * H:(g + 1) * H]
            qr[g * B:(g + 1) * B, :] = qb
            dor[g * B:(g + 1) * B, :] = ob
            qT[:, g * B:(g + 1) * B] = qb.T
            doT[:, g * B:(g + 1) * B] = ob.T
        n = counts[j]

        def block(kv, e):
            s = slots[j * NB + e]
            return kv_ref[s // 2, kv, pl.ds(pl.multiple_of((s % 2) * B, B), B), :]

        def first(e, acc, diag):
            r, d = acc
            s = jnp.dot(block(0, e), qT[...], preferred_element_type=f32)
            x = jnp.exp2(s * C2)
            if diag:
                key = lax.broadcasted_iota(jnp.int32, (B, R), 0)
                qry = lax.broadcasted_iota(jnp.int32, (B, R), 1) % B
                x = jnp.where(key <= qry, x, 0.0)
            e_buf[e] = x
            p = jnp.dot(block(1, e), doT[...], preferred_element_type=f32)
            p_buf[e] = p
            r = r + jnp.sum(x.reshape(B // 8, 8, R), 0)
            d = d + jnp.sum((x * p).reshape(B // 8, 8, R), 0)
            return r, d

        z = jnp.zeros((8, R), f32)
        acc = first(0, (z, z), True)
        r, d = lax.fori_loop(1, n, lambda e, a: first(e, a, False), acc)
        rinv = 1.0 / jnp.sum(r, 0, keepdims=True)
        delta = jnp.sum(d, 0, keepdims=True) * rinv
        dqT[...] = jnp.zeros_like(dqT)

        def second(e, _):
            w = e_buf[e] * rinv
            dvb[j * NB + e] = jnp.dot(w.astype(bf), dor[...], preferred_element_type=f32)
            ds = (w * (p_buf[e] - delta)).astype(bf)
            dkb[j * NB + e] = jnp.dot(ds, qr[...], preferred_element_type=f32) * SC
            dqT[...] += lax.dot_general(block(0, e), ds, (((0,), (0,)), ((), ())), preferred_element_type=f32)
            return 0

        lax.fori_loop(0, n, second, 0)
        for g in range(G):
            dq_ref[j * B:(j + 1) * B, g * H:(g + 1) * H] = (dqT[:, g * B:(g + 1) * B].T * SC).astype(bf)

    def out(s, _):
        a, b = inv[s], inv[NBLK + s]
        i = s // 2
        c, y, z = i % 2, i // 8, (i // 2) % 4
        rows = pl.ds(pl.multiple_of((s % 2) * B, B), B)
        part[c, y, z, 0, rows, :] = (dkb[a] + dkb[b]).astype(bf)
        part[c, y, z, 1, rows, :] = (dvb[a] + dvb[b]).astype(bf)
        return 0

    lax.fori_loop(0, NBLK, out, 0)


def attn(slots, counts, inv, q, do, kv):
    vm = pl.BlockSpec(memory_space=pltpu.VMEM)
    sm = pl.BlockSpec(memory_space=pltpu.SMEM)
    return pl.pallas_call(
        attn_kernel,
        out_shape=(jax.ShapeDtypeStruct((2 * B, R), bf), jax.ShapeDtypeStruct((2, 4, 4, 2, 2 * B, H), bf)),
        in_specs=[sm] * 3 + [vm] * 3,
        out_specs=[vm] * 2,
        scratch_shapes=[pltpu.VMEM((H, R), bf)] * 2 + [pltpu.VMEM((R, H), bf)] * 2
        + [pltpu.VMEM((NB, B, R), f32)] * 2 + [pltpu.VMEM((2 * NB + 1, B, H), f32)] * 2 + [pltpu.VMEM((H, R), f32)],
        compiler_params=pltpu.CompilerParams(vmem_limit_bytes=58 << 20),
    )(slots, counts, inv, q, do, kv)


def tables(key_lists, block_counts, span_table, first):
    qpos = lax.dynamic_slice_in_dim(span_table, first, 2)
    lists = key_lists[qpos]
    counts = block_counts[qpos]
    slots = jnp.argmax(span_table[None, None, :] == lists[:, :, None], -1).astype(jnp.int32)
    ent = jnp.arange(NB, dtype=jnp.int32)
    hit = (span_table[None, :, None] == lists[:, None, :]) & (ent[None, None, :] < counts[:, None, None])
    base = jnp.arange(2, dtype=jnp.int32)[:, None] * NB
    idx = jnp.where(hit.any(-1), jnp.argmax(hit, -1).astype(jnp.int32) + base, 2 * NB)
    return slots.reshape(-1), counts, idx.reshape(-1)

MESH = pl.DeviceIdType.MESH
bf = jnp.bfloat16; f32 = jnp.float32
NK = 8

def place():
    i = lax.axis_index("seq"); j = lax.axis_index("kvh")
    return i, j, i // 8, (i // 2) % 4, i % 2

def seq_of(y, z, c):
    return (y * 4 + z) * 2 + c

def zrel(z):
    return [z, z + 1 - 2 * (z % 2), (z + 2) % 4, 3 - z]

def enter(i, j, y, z, c):
    zs = zrel(z)
    barrier = pltpu.get_barrier_semaphore()
    seqs = [seq_of(y, z, 1 - c)] + [seq_of(y, zs[r], c) for r in (1, 2, 3)] + [seq_of((y + 1) % 4, z, c), seq_of((y + 3) % 4, z, c)]
    for s in seqs:
        pl.semaphore_signal(barrier, inc=1, device_id=(s, j), device_id_type=MESH)
    for d in range(1, NK):
        pl.semaphore_signal(barrier, inc=1, device_id=(i, (j + d) % NK), device_id_type=MESH)
    pl.semaphore_wait(barrier, len(seqs) + NK - 1)

def rcopy(src, dst, ss, rs, dev):
    return pltpu.make_async_remote_copy(src_ref=src, dst_ref=dst, send_sem=ss, recv_sem=rs, device_id=dev, device_id_type=MESH)

def gather_kernel(k_ref, v_ref, all_ref, tx, hs, hr, zs_, zr_, ys, yr, hfs, hfr, cs, cr):
    i, j, y, z, c = place()
    enter(i, j, y, z, c)
    zz = zrel(z)
    for h in range(NK):
        tx[h, 0] = k_ref[:, h*128:(h+1)*128]
        tx[h, 1] = v_ref[:, h*128:(h+1)*128]
    rows = pl.ds(pl.multiple_of(j * 32, 32), 32)
    ops = []
    for d in range(1, NK):
        h = (j + d) % NK
        cp = rcopy(tx.at[h], all_ref.at[i, :, rows, :], hs.at[d-1], hr.at[d-1], (i, h)); cp.start(); ops.append(cp)
    all_ref[i, 0, rows, :] = tx[j, 0]
    all_ref[i, 1, rows, :] = tx[j, 1]
    for cp in ops: cp.wait_recv()
    sends = list(ops)
    sib = (seq_of(y, z, 1 - c), j)
    up = (seq_of((y + 1) % 4, z, c), j)
    dn = (seq_of((y + 3) % 4, z, c), j)
    def send(src, dst, ss, rs, dev):
        cp = rcopy(src, dst, ss, rs, dev); cp.start(); sends.append(cp); return cp
    def chunk(yy, r):
        return all_ref.at[seq_of(yy % 4, zz[r], c)]
    n_c = [0]
    sibs = []
    def to_sib(yy, r):
        n = n_c[0]; n_c[0] += 1
        sibs.append(send(chunk(yy, r), chunk(yy, r), cs.at[n], cr.at[n], sib))
    zc, uc, dc, huc, hdc = [None]*4, [], [], [], []
    for r in range(4):
        if r == 0:
            for q in (1, 2, 3):
                zc[q] = send(chunk(y, 0), chunk(y, 0), zs_.at[q-1], zr_.at[q-1], (seq_of(y, zz[q], c), j))
        else:
            zc[r].wait_recv()
        uc.append(send(chunk(y, r), chunk(y, r), ys.at[0, r], yr.at[0, r], up))
        dc.append(send(chunk(y, r), chunk(y, r), ys.at[1, r], yr.at[1, r], dn))
        to_sib(y, r)
    for r in range(4):
        uc[r].wait_recv()
        s = seq_of((y + 3) % 4, zz[r], c)
        huc.append(send(all_ref.at[s, 0], all_ref.at[s, 0], hfs.at[0, r], hfr.at[0, r], up))
        to_sib(y + 3, r)
        dc[r].wait_recv()
        s = seq_of((y + 1) % 4, zz[r], c)
        hdc.append(send(all_ref.at[s, 1], all_ref.at[s, 1], hfs.at[1, r], hfr.at[1, r], dn))
        to_sib(y + 1, r)
    for r in range(4):
        huc[r].wait_recv()
        hdc[r].wait_recv()
        to_sib(y + 2, r)
    for cp in sibs: cp.wait_recv()
    for cp in sends: cp.wait_send()

def gather(k, v, cid=0):
    vm = pl.BlockSpec(memory_space=pltpu.VMEM)
    D = pltpu.SemaphoreType.DMA
    return pl.pallas_call(gather_kernel, out_shape=jax.ShapeDtypeStruct((32, 2, 256, 128), bf),
        in_specs=[vm, vm], out_specs=vm,
        scratch_shapes=[pltpu.VMEM((NK, 2, 32, 128), bf), D((7,)), D((7,)), D((3,)), D((3,)), D((2, 4)), D((2, 4)), D((2, 4)), D((2, 4)), D((16,)), D((16,))],
        compiler_params=pltpu.CompilerParams(collective_id=cid, has_side_effects=True, vmem_limit_bytes=32 << 20))(k, v)

ORDER = (1, 2, 3, 0)

def reduce_kernel(part, ko_ref, vo_ref, rx0, acc, rxa, rxb, rxz, zsrc, res, rxh,
                  s0, r0, sa, ra, sb, rb, sz, rz, sh, rh):
    i, j, y, z, c = place()
    enter(i, j, y, z, c)
    zz = zrel(z)
    yy = [(y + 2) % 4, (y + 1) % 4, (y + 3) % 4, y]
    sib = (seq_of(y, z, 1 - c), j)
    up = (seq_of(yy[1], z, c), j)
    dn = (seq_of(yy[2], z, c), j)
    sends = []
    def send(src, dst, ss, rs, dev):
        cp = rcopy(src, dst, ss, rs, dev); cp.start(); sends.append(cp); return cp
    c0 = [send(part.at[1 - c, yy[g]], rx0.at[g], s0.at[g], r0.at[g], sib) for g in range(4)]
    def tiles(fn):
        def body(t, _):
            fn(pl.ds(pl.multiple_of(t * 64, 64), 64)); return 0
        lax.fori_loop(0, 4, body, 0)
    def base(g, r):
        def one(sl):
            for kv in range(2):
                acc[g, r, kv, sl, :] = (part[c, yy[g], zz[r], kv, sl, :].astype(f32) + rx0[g, zz[r], kv, sl, :].astype(f32)).astype(bf)
        tiles(one)
    c0[0].wait_recv()
    ca = [[None]*4, [None]*4]
    for r in ORDER:
        base(0, r)
        ca[0][r] = send(acc.at[0, r, 0], rxa.at[0, r], sa.at[0, r], ra.at[0, r], up)
        ca[1][r] = send(acc.at[0, r, 1], rxa.at[1, r], sa.at[1, r], ra.at[1, r], dn)
    cb = {}
    c0[1].wait_recv()
    c0[2].wait_recv()
    for r in ORDER:
        base(1, r)
        cb[0, r, 1] = send(acc.at[1, r, 1], rxb.at[0, r, 1], sb.at[0, r, 1], rb.at[0, r, 1], up)
        base(2, r)
        cb[1, r, 0] = send(acc.at[2, r, 0], rxb.at[1, r, 0], sb.at[1, r, 0], rb.at[1, r, 0], dn)
    for r in ORDER:
        ca[0][r].wait_recv()
        def addk(sl, r=r):
            acc[1, r, 0, sl, :] = (acc[1, r, 0, sl, :].astype(f32) + rxa[0, r, sl, :].astype(f32)).astype(bf)
        tiles(addk)
        cb[0, r, 0] = send(acc.at[1, r, 0], rxb.at[0, r, 0], sb.at[0, r, 0], rb.at[0, r, 0], up)
        ca[1][r].wait_recv()
        def addv(sl, r=r):
            acc[2, r, 1, sl, :] = (acc[2, r, 1, sl, :].astype(f32) + rxa[1, r, sl, :].astype(f32)).astype(bf)
        tiles(addv)
        cb[1, r, 1] = send(acc.at[2, r, 1], rxb.at[1, r, 1], sb.at[1, r, 1], rb.at[1, r, 1], dn)
    c0[3].wait_recv()
    cz = [None] * 4
    for r in ORDER:
        for side in range(2):
            for kv in range(2):
                cb[side, r, kv].wait_recv()
        def total(sl, r=r):
            for kv in range(2):
                t = part[c, y, zz[r], kv, sl, :].astype(f32) + rx0[3, zz[r], kv, sl, :].astype(f32) + rxb[0, r, kv, sl, :].astype(f32) + rxb[1, r, kv, sl, :].astype(f32)
                if r: acc[3, r, kv, sl, :] = t.astype(bf)
                else: zsrc[kv, sl, :] = t
        tiles(total)
        if r: cz[r] = send(acc.at[3, r], rxz.at[r-1], sz.at[r-1], rz.at[r-1], (seq_of(y, zz[r], c), j))
    for r in (1, 2, 3): cz[r].wait_recv()
    for h in range(NK):
        for kv in range(2):
            sl = slice(h*32, h*32+32)
            t = zsrc[kv, sl, :]
            for r in range(3): t = t + rxz[r, kv, sl, :].astype(f32)
            res[h, kv] = t.astype(bf)
    ch = []
    for d in range(1, NK):
        h = (j + d) % NK
        ch.append(send(res.at[h], rxh.at[NK - d], sh.at[d-1], rh.at[d-1], (i, h)))
    for d in range(NK):
        src = (j + d) % NK
        col = pl.ds(pl.multiple_of(src * 128, 128), 128)
        if d == 0:
            ko_ref[:, col] = res[j, 0]
            vo_ref[:, col] = res[j, 1]
        else:
            ch[NK - d - 1].wait_recv()
            ko_ref[:, col] = rxh[d, 0]
            vo_ref[:, col] = rxh[d, 1]
    for cp in sends: cp.wait_send()

def reduce(part, cid=1):
    vm = pl.BlockSpec(memory_space=pltpu.VMEM)
    D = pltpu.SemaphoreType.DMA
    V = pltpu.VMEM
    return pl.pallas_call(reduce_kernel, out_shape=(jax.ShapeDtypeStruct((32, 1024), bf),)*2,
        in_specs=[vm], out_specs=[vm, vm],
        scratch_shapes=[V((4, 4, 2, 256, 128), bf), V((4, 4, 2, 256, 128), bf), V((2, 4, 256, 128), bf), V((2, 4, 2, 256, 128), bf), V((3, 2, 256, 128), bf),
            V((2, 256, 128), f32), V((NK, 2, 32, 128), bf), V((NK, 2, 32, 128), bf),
            D((4,)), D((4,)), D((2, 4)), D((2, 4)), D((2, 4, 2)), D((2, 4, 2)), D((3,)), D((3,)), D((7,)), D((7,))],
        compiler_params=pltpu.CompilerParams(collective_id=cid, has_side_effects=True, vmem_limit_bytes=40 << 20))(part)


def shards(queries, key_vector_rows, value_vector_rows, output_gradient, key_lists, block_counts, span_table):
    slots, counts, inv = tables(key_lists, block_counts, span_table, lax.axis_index("seq") * 2)
    kv = gather(key_vector_rows, value_vector_rows)
    grad_queries, part = attn(slots, counts, inv, queries, output_gradient, kv)
    key_gradient, value_gradient = reduce(part)
    return (grad_queries, key_gradient, value_gradient)


def solution(mesh):
    tokens = P(("seq", "kvh"), None)
    heads = P("seq", "kvh")
    return jax.shard_map(
        shards,
        mesh=mesh,
        in_specs=(heads, tokens, tokens, heads, P(), P(), P()),
        out_specs=(heads, tokens, tokens),
        check_vma=False,
    )
```

```python
import jax
import jax.numpy as jnp
from jax import lax
from jax.experimental import pallas as pl
from jax.experimental.pallas import tpu as pltpu
from jax.sharding import PartitionSpec as P
H = 128
G = 8
B = 128
NB = 24
NP = NB // 2
NBLK = 64
NK = 8
SC = H ** -0.5
C2 = SC * 1.4426950408889634
R = G * B
bf = jnp.bfloat16
f32 = jnp.float32
MESH = pl.DeviceIdType.MESH


def table_kernel(first, lists, counts, span, slots, used, index, inverse):
    def invert(s, _):
        inverse[span[s]] = s
        index[s] = 2 * NB
        index[NBLK + s] = 2 * NB
        return 0

    lax.fori_loop(0, NBLK, invert, 0, unroll=8)
    for j in range(2):
        pos = span[first[0] + j]
        n = counts[pos]


        def entry(e, _, j=j, pos=pos, n=n):
            s = inverse[lists[e, pos]]
            slots[j * NB + e] = s
            used[j * NB + e] = jnp.where(e < n, 1.0, 0.0)

            @pl.when(e < n)
            def _():
                index[j * NBLK + s] = j * NB + e
            return 0

        lax.fori_loop(0, NB, entry, 0, unroll=4)


def tables(key_lists, block_counts, span_table):
    sm = pl.BlockSpec(memory_space=pltpu.SMEM)
    i32 = jnp.int32
    first = (lax.axis_index("seq") * 2).astype(i32).reshape(1)
    return pl.pallas_call(
        table_kernel,
        out_shape=(jax.ShapeDtypeStruct((2 * NB,), i32), jax.ShapeDtypeStruct((2 * NB,), f32), jax.ShapeDtypeStruct((2 * NBLK,), i32)),
        in_specs=[sm] * 4,
        out_specs=[sm] * 3,
        scratch_shapes=[pltpu.SMEM((NBLK,), i32)],
    )(first, key_lists.T, block_counts, span_table)


def place():
    i = lax.axis_index("seq")
    j = lax.axis_index("kvh")
    return i, j, i // 8, (i // 2) % 4, i % 2


def seq_of(y, z, c):
    return (y * 4 + z) * 2 + c


def zrel(z):
    return [z, z + 1 - 2 * (z % 2), (z + 2) % 4, 3 - z]


ORDER = (1, 2, 3, 0)


def kernel(slots, used, index, k_hbm, v_hbm, q_hbm, do_hbm, dq_ref, ko_ref, vo_ref,
           kin, vin, q_ref, do_ref, tx, ka, va, part, qT, doT, qr, dor, e_buf, p_buf, pair_buf, dqT, racc, rinv, delta,
           rx0, acc, rxa, rxb, rxz, zown, res, rxh,
           s_in, hs, hr, gz_s, gz_r, gy_s, gy_r, gf_s, gf_r, gc_s, gc_r,
           s0, r0, sa, ra, sb, rb, sz, rz, sh, rh):
    i, j, y, z, c = place()
    zz = zrel(z)
    yy = [(y + 2) % 4, (y + 1) % 4, (y + 3) % 4, y]
    sib = (seq_of(y, z, 1 - c), j)
    up = (seq_of(yy[1], z, c), j)
    dn = (seq_of(yy[2], z, c), j)
    kva = (ka, va)
    sends = []

    def send(src, dst, ss, rs, dev):
        cp = pltpu.make_async_remote_copy(src_ref=src, dst_ref=dst, send_sem=ss, recv_sem=rs, device_id=dev, device_id_type=MESH)
        cp.start()
        sends.append(cp)
        return cp

    loads = [pltpu.make_async_copy(a, b, s_in.at[n]) for n, (a, b) in enumerate(((k_hbm, kin), (v_hbm, vin), (q_hbm, q_ref), (do_hbm, do_ref)))]
    for cp in loads:
        cp.start()
    barrier = pltpu.get_barrier_semaphore()
    near = [sib, up, dn] + [(seq_of(y, zz[r], c), j) for r in (1, 2, 3)]
    for dev in near + [(i, (j + d) % NK) for d in range(1, NK)]:
        pl.semaphore_signal(barrier, inc=1, device_id=dev, device_id_type=MESH)
    loads[0].wait()
    loads[1].wait()
    for h in range(NK):
        tx[h, 0] = kin[:, h * H:(h + 1) * H]
        tx[h, 1] = vin[:, h * H:(h + 1) * H]
    pl.semaphore_wait(barrier, len(near) + NK - 1)
    rows = pl.ds(pl.multiple_of((j % 4) * 32, 32), 32)
    heads = []
    for d in range(1, NK):
        h = (j + d) % NK
        for t in range(2):
            heads.append(send(tx.at[h, t], kva[t].at[2 * i + j // 4, rows, :], hs.at[t, d - 1], hr.at[t, d - 1], (i, h)))
    for t in range(2):
        kva[t][2 * i + j // 4, rows, :] = tx[j, t]

    def gather(t):
        def chunk(yp, r):
            return kva[t].at[pl.ds(2 * seq_of(yp, zz[r], c), 2)]

        def half(yp, r, p):
            return kva[t].at[2 * seq_of(yp, zz[r], c) + p]

        cs = []

        def to_sib(yp, r):
            n = len(cs)
            cs.append(send(chunk(yp, r), chunk(yp, r), gc_s.at[t, n], gc_r.at[t, n], sib))

        uc, dc, hu, hd, zc = [], [], [], [], []

        def around(r):
            uc.append(send(chunk(y, r), chunk(y, r), gy_s.at[t, 0, r], gy_r.at[t, 0, r], up))
            dc.append(send(chunk(y, r), chunk(y, r), gy_s.at[t, 1, r], gy_r.at[t, 1, r], dn))

        around(0)
        for r in (1, 2, 3):
            zc.append(send(chunk(y, 0), chunk(y, 0), gz_s.at[t, r - 1], gz_r.at[t, r - 1], (seq_of(y, zz[r], c), j)))
        to_sib(y, 0)
        yield
        for r in (1, 2, 3):
            zc[r - 1].wait_recv()
            around(r)
            to_sib(y, r)
        yield
        for r in range(4):
            uc[r].wait_recv()
            hu.append(send(half(yy[2], r, 0), half(yy[2], r, 0), gf_s.at[t, 0, r], gf_r.at[t, 0, r], up))
            to_sib(yy[2], r)
            dc[r].wait_recv()
            hd.append(send(half(yy[1], r, 1), half(yy[1], r, 1), gf_s.at[t, 1, r], gf_r.at[t, 1, r], dn))
            to_sib(yy[1], r)
            if r == 1:
                yield
        yield
        for r in range(4):
            hu[r].wait_recv()
            hd[r].wait_recv()
            to_sib(yy[0], r)
        yield
        for cp in cs:
            cp.wait_recv()

    def add(dst, a, b, *more):
        t = a.astype(f32) + b.astype(f32)
        for m in more:
            t = t + m.astype(f32)
        return t.astype(dst)

    def reduce(t, out_ref):
        mine = part.at[t, c]
        c0 = [send(part.at[t, 1 - c, yy[g]], rx0.at[t, g], s0.at[t, g], r0.at[t, g], sib) for g in range(4)]
        yield

        def base(g, r):
            acc[t, g, r] = add(bf, mine[yy[g], zz[r]], rx0[t, g, zz[r]])

        cu, cd, bu, bd, cz = [None] * 4, [None] * 4, {}, {}, [None] * 4
        c0[0].wait_recv()
        for r in ORDER:
            base(0, r)
            cu[r] = send(acc.at[t, 0, r, 0], rxa.at[t, 0, r], sa.at[t, 0, r], ra.at[t, 0, r], up)
            cd[r] = send(acc.at[t, 0, r, 1], rxa.at[t, 1, r], sa.at[t, 1, r], ra.at[t, 1, r], dn)
        yield
        c0[1].wait_recv()
        c0[2].wait_recv()
        for r in ORDER:
            base(1, r)
            bu[r, 1] = send(acc.at[t, 1, r, 1], rxb.at[t, 0, r, 1], sb.at[t, 0, r, 1], rb.at[t, 0, r, 1], up)
            base(2, r)
            bd[r, 0] = send(acc.at[t, 2, r, 0], rxb.at[t, 1, r, 0], sb.at[t, 1, r, 0], rb.at[t, 1, r, 0], dn)
        yield
        for r in ORDER:
            cu[r].wait_recv()
            acc[t, 1, r, 0] = add(bf, acc[t, 1, r, 0], rxa[t, 0, r])
            bu[r, 0] = send(acc.at[t, 1, r, 0], rxb.at[t, 0, r, 0], sb.at[t, 0, r, 0], rb.at[t, 0, r, 0], up)
            cd[r].wait_recv()
            acc[t, 2, r, 1] = add(bf, acc[t, 2, r, 1], rxa[t, 1, r])
            bd[r, 1] = send(acc.at[t, 2, r, 1], rxb.at[t, 1, r, 1], sb.at[t, 1, r, 1], rb.at[t, 1, r, 1], dn)
        yield
        c0[3].wait_recv()
        for r in ORDER:
            for p in range(2):
                bu[r, p].wait_recv()
                bd[r, p].wait_recv()
            if r:
                acc[t, 3, r] = add(bf, mine[y, zz[r]], rx0[t, 3, zz[r]], rxb[t, 0, r], rxb[t, 1, r])
                cz[r] = send(acc.at[t, 3, r], rxz.at[t, r - 1], sz.at[t, r - 1], rz.at[t, r - 1], (seq_of(y, zz[r], c), j))
            else:
                zown[t] = add(f32, mine[y, z], rx0[t, 3, z], rxb[t, 0, 0], rxb[t, 1, 0])
        yield
        for r in (1, 2, 3):
            cz[r].wait_recv()
        for h in range(NK):
            p, sl = h // 4, slice((h % 4) * 32, (h % 4) * 32 + 32)
            res[t, h] = add(bf, zown[t, p, sl, :], rxz[t, 0, p, sl, :], rxz[t, 1, p, sl, :], rxz[t, 2, p, sl, :])
        ch = []
        for d in range(1, NK):
            h = (j + d) % NK
            ch.append(send(res.at[t, h], rxh.at[t, NK - d], sh.at[t, d - 1], rh.at[t, d - 1], (i, h)))
        yield
        for d in range(NK):
            col = pl.ds(pl.multiple_of(((j + d) % NK) * H, H), H)
            if d == 0:
                out_ref[:, col] = res[t, j]
            else:
                ch[NK - d - 1].wait_recv()
                out_ref[:, col] = rxh[t, d]

    def advance(flow, n=1):
        for _ in range(n):
            next(flow, None)

    def prepare(b):
        for g in range(G):
            qb = q_ref[b * B:(b + 1) * B, g * H:(g + 1) * H]
            ob = do_ref[b * B:(b + 1) * B, g * H:(g + 1) * H]
            qr[b, g * B:(g + 1) * B, :] = qb
            dor[b, g * B:(g + 1) * B, :] = ob
            qT[b, :, g * B:(g + 1) * B] = qb.T
            doT[b, :, g * B:(g + 1) * B] = ob.T

    def two(t, b, n):
        got = []
        for p in range(2):
            got.append(kva[t][slots[b * NB + 2 * n + p]])
        return jnp.concatenate(got, 0)

    def loop(lo, hi, fn):
        def body(n, _):
            fn(n)
            return 0
        lax.fori_loop(lo, hi, body, 0)

    def scores(b, lo, hi):
        def one(n, first=False):
            s = jnp.dot(two(0, b, n), qT[b], preferred_element_type=f32)
            for p in range(2):
                x = jnp.exp2(s[p * B:(p + 1) * B] * C2)
                if first and p == 0:
                    key = lax.broadcasted_iota(jnp.int32, (B, R), 0)
                    qry = lax.broadcasted_iota(jnp.int32, (B, R), 1) % B
                    x = jnp.where(key <= qry, x, 0.0)
                e_buf[b, n, p * B:(p + 1) * B, :] = x
                t = jnp.sum(x.reshape(B // 8, 8, R), 0) * used[b * NB + 2 * n + p]
                if first and p == 0:
                    racc[b] = t
                else:
                    racc[b] += t
        if lo == 0:
            one(0, True)
            lo = 1
        loop(lo, hi, one)
        if hi == NP:
            rinv[b] = jnp.broadcast_to(1.0 / jnp.sum(racc[b], 0, keepdims=True), (8, R))

    def weights(b, n):
        return jnp.concatenate([e_buf[b, n, p * B:(p + 1) * B, :] * (rinv[b, 0:1, :] * used[b * NB + 2 * n + p]) for p in range(2)], 0)

    def values(b, lo, hi):
        def one(n):
            w = weights(b, n).astype(bf)
            o = jnp.dot(w, dor[b], preferred_element_type=f32)
            for p in range(2):
                pair_buf[b * NB + 2 * n + p] = o[p * B:(p + 1) * B]
        loop(lo, hi, one)

    def products(b, lo, hi):
        def one(n):
            p = jnp.dot(two(1, b, n), doT[b], preferred_element_type=f32)
            p_buf[n] = p
            for h in range(2):
                sl = slice(h * B, h * B + B)
                racc[b] += jnp.sum((e_buf[b, n, sl, :] * p[sl]).reshape(B // 8, 8, R), 0) * used[b * NB + 2 * n + h]
        if lo == 0:
            racc[b] = jnp.zeros((8, R), f32)
        loop(lo, hi, one)
        if hi == NP:
            delta[b] = jnp.broadcast_to(jnp.sum(racc[b], 0, keepdims=True) * rinv[b, 0:1, :], (8, R))
            dqT[...] = jnp.zeros_like(dqT)

    def grads(b, lo, hi):
        def one(n):
            w = weights(b, n)
            ds = (w * (p_buf[n] - delta[b, 0:1, :])).astype(bf)
            o = jnp.dot(ds, qr[b], preferred_element_type=f32)
            for p in range(2):
                pair_buf[b * NB + 2 * n + p] = o[p * B:(p + 1) * B]
            dqT[...] += lax.dot_general(two(0, b, n), ds, (((0,), (0,)), ((), ())), preferred_element_type=f32)
        loop(lo, hi, one)
        if hi == NP:
            for g in range(G):
                dq_ref[b * B:(b + 1) * B, g * H:(g + 1) * H] = (dqT[:, g * B:(g + 1) * B].T * SC).astype(bf)

    def collect(t, scale):
        def one(s):
            i_ = s // 2
            v = pair_buf[index[s]] + pair_buf[index[NBLK + s]]
            if scale != 1.0:
                v = v * scale
            part[t, i_ % 2, i_ // 8, (i_ // 2) % 4, s % 2] = v.astype(bf)
        loop(0, NBLK, one)

    pair_buf[2 * NB] = jnp.zeros((B, H), f32)
    loads[2].wait()
    loads[3].wait()
    prepare(0)
    for cp in heads:
        cp.wait_recv()
    kf, vf = gather(0), gather(1)
    advance(kf)
    prepare(1)
    advance(kf)
    advance(vf)
    advance(kf, 2)
    advance(vf)
    advance(kf, 2)
    scores(0, 0, 6)
    advance(vf)
    scores(0, 6, NP)
    advance(vf)
    values(0, 0, 6)
    advance(vf)
    values(0, 6, NP)
    scores(1, 0, NP)
    values(1, 0, NP)
    advance(vf)
    collect(1, 1.0)
    vr = reduce(1, vo_ref)
    advance(vr)
    products(0, 0, 6)
    advance(vr)
    products(0, 6, NP)
    advance(vr)
    grads(0, 0, 6)
    advance(vr)
    grads(0, 6, NP)
    products(1, 0, 6)
    advance(vr)
    products(1, 6, NP)
    grads(1, 0, 6)
    advance(vr)
    grads(1, 6, NP)
    collect(0, SC)
    kr = reduce(0, ko_ref)
    advance(kr, 2)
    advance(vr)
    for _ in kr:
        pass
    for cp in sends:
        cp.wait_send()


def fused(slots, used, index, k, v, q, do):
    vm = pl.BlockSpec(memory_space=pltpu.VMEM)
    sm = pl.BlockSpec(memory_space=pltpu.SMEM)
    hb = pl.BlockSpec(memory_space=pl.ANY)
    V = pltpu.VMEM
    D = pltpu.SemaphoreType.DMA
    tok = jax.ShapeDtypeStruct((32, NK * H), bf)
    return pl.pallas_call(
        kernel,
        out_shape=(jax.ShapeDtypeStruct((2 * B, R), bf), tok, tok),
        in_specs=[sm] * 3 + [hb] * 4,
        out_specs=[vm] * 3,
        scratch_shapes=[
            V((32, NK * H), bf), V((32, NK * H), bf), V((2 * B, R), bf), V((2 * B, R), bf),
            V((NK, 2, 32, H), bf), V((NBLK, B, H), bf), V((NBLK, B, H), bf), V((2, 2, 4, 4, 2, B, H), bf),
            V((2, H, R), bf), V((2, H, R), bf), V((2, R, H), bf), V((2, R, H), bf),
            V((2, NP, 2 * B, R), f32), V((NP, 2 * B, R), f32), V((2 * NB + 1, B, H), f32), V((H, R), f32),
            V((2, 8, R), f32), V((2, 8, R), f32), V((2, 8, R), f32),
            V((2, 4, 4, 2, B, H), bf), V((2, 4, 4, 2, B, H), bf), V((2, 2, 4, B, H), bf), V((2, 2, 4, 2, B, H), bf),
            V((2, 3, 2, B, H), bf), V((2, 2, B, H), f32), V((2, NK, 32, H), bf), V((2, NK, 32, H), bf),
            D((4,)), D((2, 7)), D((2, 7)), D((2, 3)), D((2, 3)), D((2, 2, 4)), D((2, 2, 4)), D((2, 2, 4)), D((2, 2, 4)), D((2, 16)), D((2, 16)),
            D((2, 4)), D((2, 4)), D((2, 2, 4)), D((2, 2, 4)), D((2, 2, 4, 2)), D((2, 2, 4, 2)), D((2, 3)), D((2, 3)), D((2, 7)), D((2, 7)),
        ],
        compiler_params=pltpu.CompilerParams(collective_id=0, has_side_effects=True, vmem_limit_bytes=62 << 20),
    )(slots, used, index, k, v, q, do)


def shards(queries, key_vector_rows, value_vector_rows, output_gradient, key_lists, block_counts, span_table):
    slots, used, index = tables(key_lists, block_counts, span_table)
    return fused(slots, used, index, key_vector_rows, value_vector_rows, queries, output_gradient)


def solution(mesh):
    tokens = P(("seq", "kvh"), None)
    heads = P("seq", "kvh")
    return jax.shard_map(
        shards,
        mesh=mesh,
        in_specs=(heads, tokens, tokens, heads, P(), P(), P()),
        out_specs=(heads, tokens, tokens),
        check_vma=False,
    )
```

```python
import jax
import jax.numpy as jnp
from jax import lax
from jax.experimental import pallas as pl
from jax.experimental.pallas import tpu as pltpu
from jax.sharding import PartitionSpec as P
H = 128
G = 8
B = 128
NB = 24
NP = NB // 2
NBLK = 64
NK = 8
SC = H ** -0.5
C2 = SC * 1.4426950408889634
R = G * B
bf = jnp.bfloat16
f32 = jnp.float32
MESH = pl.DeviceIdType.MESH
UNROLL = 3


def table_kernel(first, lists, counts, span, slots, used, index, inverse):
    def invert(s, _):
        inverse[span[s]] = s
        index[s] = 2 * NB
        index[NBLK + s] = 2 * NB
        return 0

    lax.fori_loop(0, NBLK, invert, 0, unroll=8)
    for j in range(2):
        pos = span[first[0] + j]
        n = counts[pos]


        def entry(e, _, j=j, pos=pos, n=n):
            s = inverse[lists[e, pos]]
            slots[j * NB + e] = s
            used[j * NB + e] = jnp.where(e < n, 1.0, 0.0)

            @pl.when(e < n)
            def _():
                index[j * NBLK + s] = j * NB + e
            return 0

        lax.fori_loop(0, NB, entry, 0, unroll=4)


def tables(key_lists, block_counts, span_table):
    sm = pl.BlockSpec(memory_space=pltpu.SMEM)
    i32 = jnp.int32
    first = (lax.axis_index("seq") * 2).astype(i32).reshape(1)
    return pl.pallas_call(
        table_kernel,
        out_shape=(jax.ShapeDtypeStruct((2 * NB,), i32), jax.ShapeDtypeStruct((2 * NB,), f32), jax.ShapeDtypeStruct((2 * NBLK,), i32)),
        in_specs=[sm] * 4,
        out_specs=[sm] * 3,
        scratch_shapes=[pltpu.SMEM((NBLK,), i32)],
    )(first, key_lists.T, block_counts, span_table)


def place():
    i = lax.axis_index("seq")
    j = lax.axis_index("kvh")
    return i, j, i // 8, (i // 2) % 4, i % 2


def seq_of(y, z, c):
    return (y * 4 + z) * 2 + c


def zrel(z):
    return [z, z + 1 - 2 * (z % 2), (z + 2) % 4, 3 - z]


ORDER = (1, 2, 3, 0)


def kernel(slots, used, index, k_hbm, v_hbm, q_hbm, do_hbm, dq_ref, ko_ref, vo_ref,
           kin, vin, q_ref, do_ref, tx, ka, va, part, qT, doT, qr, dor, e_buf, p_buf, pair_buf, dqT, racc, rinv, delta,
           rx0, acc, rxb, rxz, zown, res, rxh,
           s_in, hs, hr, gz_s, gz_r, gy_s, gy_r, gf_s, gf_r, gc_s, gc_r,
           s0, r0, sb, rb, sz, rz, sh, rh):
    i, j, y, z, c = place()
    zz = zrel(z)
    yy = [(y + 2) % 4, (y + 1) % 4, (y + 3) % 4, y]
    sib = (seq_of(y, z, 1 - c), j)
    up = (seq_of(yy[1], z, c), j)
    dn = (seq_of(yy[2], z, c), j)
    kva = (ka, va)
    sends = []

    def send(src, dst, ss, rs, dev):
        cp = pltpu.make_async_remote_copy(src_ref=src, dst_ref=dst, send_sem=ss, recv_sem=rs, device_id=dev, device_id_type=MESH)
        cp.start()
        sends.append(cp)
        return cp

    loads = [pltpu.make_async_copy(a, b, s_in.at[n]) for n, (a, b) in enumerate(((k_hbm, kin), (v_hbm, vin), (q_hbm, q_ref), (do_hbm, do_ref)))]
    for cp in loads:
        cp.start()
    barrier = pltpu.get_barrier_semaphore()
    near = [sib, up, dn, (seq_of(yy[0], z, c), j)] + [(seq_of(y, zz[r], c), j) for r in (1, 2, 3)]
    for dev in near + [(i, (j + d) % NK) for d in range(1, NK)]:
        pl.semaphore_signal(barrier, inc=1, device_id=dev, device_id_type=MESH)
    loads[0].wait()
    loads[1].wait()
    for h in range(NK):
        tx[h, 0] = kin[:, h * H:(h + 1) * H]
        tx[h, 1] = vin[:, h * H:(h + 1) * H]
    pl.semaphore_wait(barrier, len(near) + NK - 1)
    rows = pl.ds(pl.multiple_of((j % 4) * 32, 32), 32)
    heads = []
    for d in range(1, NK):
        h = (j + d) % NK
        for t in range(2):
            heads.append(send(tx.at[h, t], kva[t].at[2 * i + j // 4, rows, :], hs.at[t, d - 1], hr.at[t, d - 1], (i, h)))
    for t in range(2):
        kva[t][2 * i + j // 4, rows, :] = tx[j, t]

    def gather(t):
        def chunk(yp, r):
            return kva[t].at[pl.ds(2 * seq_of(yp, zz[r], c), 2)]

        def half(yp, r, p):
            return kva[t].at[2 * seq_of(yp, zz[r], c) + p]

        cs = []

        def to_sib(yp, r):
            n = len(cs)
            cs.append(send(chunk(yp, r), chunk(yp, r), gc_s.at[t, n], gc_r.at[t, n], sib))

        uc, dc, hu, hd, zc = [], [], [], [], []

        def around(r):
            uc.append(send(chunk(y, r), chunk(y, r), gy_s.at[t, 0, r], gy_r.at[t, 0, r], up))
            dc.append(send(chunk(y, r), chunk(y, r), gy_s.at[t, 1, r], gy_r.at[t, 1, r], dn))

        if t == 0:
            around(0)
        for r in (1, 2, 3):
            zc.append(send(chunk(y, 0), chunk(y, 0), gz_s.at[t, r - 1], gz_r.at[t, r - 1], (seq_of(y, zz[r], c), j)))
        to_sib(y, 0)
        yield
        if t == 1:
            around(0)
        for r in (1, 2, 3):
            zc[r - 1].wait_recv()
            around(r)
            to_sib(y, r)
        yield
        for r in range(4):
            uc[r].wait_recv()
            hu.append(send(half(yy[2], r, 0), half(yy[2], r, 0), gf_s.at[t, 0, r], gf_r.at[t, 0, r], up))
            to_sib(yy[2], r)
            dc[r].wait_recv()
            hd.append(send(half(yy[1], r, 1), half(yy[1], r, 1), gf_s.at[t, 1, r], gf_r.at[t, 1, r], dn))
            to_sib(yy[1], r)
            if r == 1:
                yield
        yield
        for r in range(4):
            hu[r].wait_recv()
            hd[r].wait_recv()
            to_sib(yy[0], r)
        yield
        for cp in cs:
            cp.wait_recv()

    def add(dst, a, b, *more):
        t = a.astype(f32) + b.astype(f32)
        for m in more:
            t = t + m.astype(f32)
        return t.astype(dst)

    def reduce(t, out_ref):
        mine = part.at[t, c]
        c0, cb, cz = [None] * 4, {}, [None] * 4
        for r in ORDER:
            c0[r] = send(part.at[t, 1 - c, :, zz[r]], rx0.at[t, r], s0.at[t, r], r0.at[t, r], sib)
        yield
        for r in ORDER:
            c0[r].wait_recv()
            for g in range(3):
                acc[t, g, r] = add(bf, mine[yy[g], zz[r]], rx0[t, r, yy[g]])
                cb[g, r] = send(acc.at[t, g, r], rxb.at[t, g, r], sb.at[t, g, r], rb.at[t, g, r], (seq_of(yy[g], z, c), j))
        yield
        for r in ORDER:
            for g in range(3):
                cb[g, r].wait_recv()
            if r:
                acc[t, 3, r] = add(bf, mine[y, zz[r]], rx0[t, r, y], rxb[t, 0, r], rxb[t, 1, r], rxb[t, 2, r])
                cz[r] = send(acc.at[t, 3, r], rxz.at[t, r - 1], sz.at[t, r - 1], rz.at[t, r - 1], (seq_of(y, zz[r], c), j))
                if r == 2:
                    yield
            else:
                zown[t] = add(f32, mine[y, z], rx0[t, 0, y], rxb[t, 0, 0], rxb[t, 1, 0], rxb[t, 2, 0])
        yield
        for r in (1, 2, 3):
            cz[r].wait_recv()
        for h in range(NK):
            p, sl = h // 4, slice((h % 4) * 32, (h % 4) * 32 + 32)
            res[t, h] = add(bf, zown[t, p, sl, :], rxz[t, 0, p, sl, :], rxz[t, 1, p, sl, :], rxz[t, 2, p, sl, :])
        ch = []
        for d in range(1, NK):
            h = (j + d) % NK
            ch.append(send(res.at[t, h], rxh.at[t, NK - d], sh.at[t, d - 1], rh.at[t, d - 1], (i, h)))
        yield
        for d in range(NK):
            col = pl.ds(pl.multiple_of(((j + d) % NK) * H, H), H)
            if d == 0:
                out_ref[:, col] = res[t, j]
            else:
                ch[NK - d - 1].wait_recv()
                out_ref[:, col] = rxh[t, d]

    def advance(flow, n=1):
        for _ in range(n):
            next(flow, None)

    def prepare(b):
        for g in range(G):
            qb = q_ref[b * B:(b + 1) * B, g * H:(g + 1) * H]
            ob = do_ref[b * B:(b + 1) * B, g * H:(g + 1) * H]
            qr[b, g * B:(g + 1) * B, :] = qb
            dor[b, g * B:(g + 1) * B, :] = ob
            qT[b, :, g * B:(g + 1) * B] = qb.T
            doT[b, :, g * B:(g + 1) * B] = ob.T

    def two(t, b, n):
        got = []
        for p in range(2):
            got.append(kva[t][slots[b * NB + 2 * n + p]])
        return jnp.concatenate(got, 0)

    def loop(lo, hi, fn, unroll=UNROLL):
        def body(n, _):
            fn(n)
            return 0
        lax.fori_loop(lo, hi, body, 0, unroll=unroll)

    def scores(b, lo, hi):
        def one(n, first=False):
            s = jnp.dot(two(0, b, n), qT[b], preferred_element_type=f32)
            for p in range(2):
                x = jnp.exp2(s[p * B:(p + 1) * B] * C2)
                if first and p == 0:
                    key = lax.broadcasted_iota(jnp.int32, (B, R), 0)
                    qry = lax.broadcasted_iota(jnp.int32, (B, R), 1) % B
                    x = jnp.where(key <= qry, x, 0.0)
                e_buf[b, n, p * B:(p + 1) * B, :] = x
                t = jnp.sum(x.reshape(B // 8, 8, R), 0) * used[b * NB + 2 * n + p]
                if first and p == 0:
                    racc[b] = t
                else:
                    racc[b] += t
        if lo == 0:
            one(0, True)
            lo = 1
        loop(lo, hi, one)
        if hi == NP:
            rinv[b] = jnp.broadcast_to(1.0 / jnp.sum(racc[b], 0, keepdims=True), (8, R))

    def weights(b, n):
        return jnp.concatenate([e_buf[b, n, p * B:(p + 1) * B, :] * (rinv[b, 0:1, :] * used[b * NB + 2 * n + p]) for p in range(2)], 0)

    def values(b, lo, hi):
        def one(n):
            w = weights(b, n).astype(bf)
            o = jnp.dot(w, dor[b], preferred_element_type=f32)
            for p in range(2):
                pair_buf[b * NB + 2 * n + p] = o[p * B:(p + 1) * B]
        loop(lo, hi, one)

    def products(b, lo, hi):
        def one(n):
            p = jnp.dot(two(1, b, n), doT[b], preferred_element_type=f32)
            p_buf[n] = p
            for h in range(2):
                sl = slice(h * B, h * B + B)
                racc[b] += jnp.sum((e_buf[b, n, sl, :] * p[sl]).reshape(B // 8, 8, R), 0) * used[b * NB + 2 * n + h]
        if lo == 0:
            racc[b] = jnp.zeros((8, R), f32)
        loop(lo, hi, one)
        if hi == NP:
            delta[b] = jnp.broadcast_to(jnp.sum(racc[b], 0, keepdims=True) * rinv[b, 0:1, :], (8, R))

    def grads(b, lo, hi):
        def one(n):
            w = weights(b, n)
            ds = (w * (p_buf[n] - delta[b, 0:1, :])).astype(bf)
            o = jnp.dot(ds, qr[b], preferred_element_type=f32)
            for p in range(2):
                pair_buf[b * NB + 2 * n + p] = o[p * B:(p + 1) * B]
            e_buf[b, n] = ds.astype(f32)
        loop(lo, hi, one)

    def queries(b, lo, hi):
        def one(n):
            dqT[...] += lax.dot_general(two(0, b, n), e_buf[b, n].astype(bf), (((0,), (0,)), ((), ())), preferred_element_type=f32)
        if lo == 0:
            dqT[...] = jnp.zeros_like(dqT)
        loop(lo, hi, one)
        if hi == NP:
            for g in range(G):
                dq_ref[b * B:(b + 1) * B, g * H:(g + 1) * H] = (dqT[:, g * B:(g + 1) * B].T * SC).astype(bf)

    def collect(t, scale):
        def one(s):
            i_ = s // 2
            v = pair_buf[index[s]] + pair_buf[index[NBLK + s]]
            if scale != 1.0:
                v = v * scale
            part[t, i_ % 2, i_ // 8, (i_ // 2) % 4, s % 2] = v.astype(bf)
        loop(0, NBLK, one)

    pair_buf[2 * NB] = jnp.zeros((B, H), f32)
    loads[2].wait()
    loads[3].wait()
    prepare(0)
    for cp in heads:
        cp.wait_recv()
    kf, vf = gather(0), gather(1)
    advance(kf)
    prepare(1)
    advance(kf)
    advance(vf)
    advance(kf, 2)
    advance(vf)
    advance(kf, 2)
    scores(0, 0, NP)
    advance(vf)
    values(0, 0, NP)
    advance(vf)
    scores(1, 0, NP)
    advance(vf)
    values(1, 0, NP)
    collect(1, 1.0)
    vr = reduce(1, vo_ref)
    advance(vr)
    advance(vf)
    products(0, 0, NP)
    advance(vr)
    grads(0, 0, NP)
    products(1, 0, NP)
    grads(1, 0, NP)
    collect(0, SC)
    kr = reduce(0, ko_ref)
    advance(kr)
    advance(vr)
    queries(0, 0, NP)
    advance(kr)
    advance(vr)
    queries(1, 0, NP)
    advance(vr)
    advance(kr, 2)
    advance(vr)
    for _ in kr:
        pass
    for _ in vr:
        pass
    for cp in sends:
        cp.wait_send()


def fused(slots, used, index, k, v, q, do):
    vm = pl.BlockSpec(memory_space=pltpu.VMEM)
    sm = pl.BlockSpec(memory_space=pltpu.SMEM)
    hb = pl.BlockSpec(memory_space=pl.ANY)
    V = pltpu.VMEM
    D = pltpu.SemaphoreType.DMA
    tok = jax.ShapeDtypeStruct((32, NK * H), bf)
    return pl.pallas_call(
        kernel,
        out_shape=(jax.ShapeDtypeStruct((2 * B, R), bf), tok, tok),
        in_specs=[sm] * 3 + [hb] * 4,
        out_specs=[vm] * 3,
        scratch_shapes=[
            V((32, NK * H), bf), V((32, NK * H), bf), V((2 * B, R), bf), V((2 * B, R), bf),
            V((NK, 2, 32, H), bf), V((NBLK, B, H), bf), V((NBLK, B, H), bf), V((2, 2, 4, 4, 2, B, H), bf),
            V((2, H, R), bf), V((2, H, R), bf), V((2, R, H), bf), V((2, R, H), bf),
            V((2, NP, 2 * B, R), f32), V((NP, 2 * B, R), f32), V((2 * NB + 1, B, H), f32), V((H, R), f32),
            V((2, 8, R), f32), V((2, 8, R), f32), V((2, 8, R), f32),
            V((2, 4, 4, 2, B, H), bf), V((2, 4, 4, 2, B, H), bf), V((2, 3, 4, 2, B, H), bf),
            V((2, 3, 2, B, H), bf), V((2, 2, B, H), f32), V((2, NK, 32, H), bf), V((2, NK, 32, H), bf),
            D((4,)), D((2, 7)), D((2, 7)), D((2, 3)), D((2, 3)), D((2, 2, 4)), D((2, 2, 4)), D((2, 2, 4)), D((2, 2, 4)), D((2, 16)), D((2, 16)),
            D((2, 4)), D((2, 4)), D((2, 3, 4)), D((2, 3, 4)), D((2, 3)), D((2, 3)), D((2, 7)), D((2, 7)),
        ],
        compiler_params=pltpu.CompilerParams(collective_id=0, has_side_effects=True, vmem_limit_bytes=62 << 20),
    )(slots, used, index, k, v, q, do)


def shards(queries, key_vector_rows, value_vector_rows, output_gradient, key_lists, block_counts, span_table):
    slots, used, index = tables(key_lists, block_counts, span_table)
    return fused(slots, used, index, key_vector_rows, value_vector_rows, queries, output_gradient)


def solution(mesh):
    tokens = P(("seq", "kvh"), None)
    heads = P("seq", "kvh")
    return jax.shard_map(
        shards,
        mesh=mesh,
        in_specs=(heads, tokens, tokens, heads, P(), P(), P()),
        out_specs=(heads, tokens, tokens),
        check_vma=False,
    )
```

```python
import jax
import jax.numpy as jnp
from jax import lax
from jax.experimental import pallas as pl
from jax.experimental.pallas import tpu as pltpu
from jax.sharding import PartitionSpec as P
H = 128
G = 8
B = 128
NB = 24
NP = NB // 2
NBLK = 64
NK = 8
SC = H ** -0.5
C2 = SC * 1.4426950408889634
R = G * B
bf = jnp.bfloat16
f32 = jnp.float32
MESH = pl.DeviceIdType.MESH
UNROLL = 3


def place():
    i = lax.axis_index("seq")
    j = lax.axis_index("kvh")
    return i, j, i // 8, (i // 2) % 4, i % 2


def seq_of(y, z, c):
    return (y * 4 + z) * 2 + c


def zrel(z):
    return [z, z + 1 - 2 * (z % 2), (z + 2) % 4, 3 - z]


ORDER = (1, 2, 3, 0)


def kernel(lists_hbm, counts_hbm, span_hbm, row_hbm, k_hbm, v_hbm, q_hbm, do_hbm, dq_ref, ko_ref, vo_ref,
           lists, counts, span, row, tab_v, tab, kin, vin, q_ref, do_ref, tx, ka, va, part, qT, doT, qr, dor, e_buf, p_buf, pair_buf, dqT, racc, rinv, delta,
           rx0, acc, rxb, rxz, zown, res, rxh,
           s_in, hs, hr, gz_s, gz_r, gy_s, gy_r, gf_s, gf_r, gc_s, gc_r,
           s0, r0, sb, rb, sz, rz, sh, rh):
    i, j, y, z, c = place()
    zz = zrel(z)
    yy = [(y + 2) % 4, (y + 1) % 4, (y + 3) % 4, y]
    sib = (seq_of(y, z, 1 - c), j)
    up = (seq_of(yy[1], z, c), j)
    dn = (seq_of(yy[2], z, c), j)
    kva = (ka, va)
    sends = []

    def send(src, dst, ss, rs, dev):
        cp = pltpu.make_async_remote_copy(src_ref=src, dst_ref=dst, send_sem=ss, recv_sem=rs, device_id=dev, device_id_type=MESH)
        cp.start()
        sends.append(cp)
        return cp

    barrier = pltpu.get_barrier_semaphore()
    near = [sib, up, dn, (seq_of(yy[0], z, c), j)] + [(seq_of(y, zz[r], c), j) for r in (1, 2, 3)]
    for dev in near + [(i, (j + d) % NK) for d in range(1, NK)]:
        pl.semaphore_signal(barrier, inc=1, device_id=dev, device_id_type=MESH)
    loads = [pltpu.make_async_copy(a, b, s_in.at[n]) for n, (a, b) in enumerate(((k_hbm, kin), (v_hbm, vin), (q_hbm, q_ref), (do_hbm, do_ref), (lists_hbm, lists), (counts_hbm, counts), (span_hbm, span), (row_hbm, row)))]
    for cp in loads:
        cp.start()
    loads[0].wait()
    loads[1].wait()
    for h in range(NK):
        tx[h, 0] = kin[:, h * H:(h + 1) * H]
        tx[h, 1] = vin[:, h * H:(h + 1) * H]
    pl.semaphore_wait(barrier, len(near) + NK - 1)
    rows = pl.ds(pl.multiple_of((j % 4) * 32, 32), 32)
    heads = []
    for d in range(1, NK):
        h = (j + d) % NK
        for t in range(2):
            heads.append(send(tx.at[h, t], kva[t].at[2 * i + j // 4, rows, :], hs.at[t, d - 1], hr.at[t, d - 1], (i, h)))
    for t in range(2):
        kva[t][2 * i + j // 4, rows, :] = tx[j, t]

    def gather(t):
        def chunk(yp, r):
            return kva[t].at[pl.ds(2 * seq_of(yp, zz[r], c), 2)]

        def half(yp, r, p):
            return kva[t].at[2 * seq_of(yp, zz[r], c) + p]

        cs = []

        def to_sib(yp, r):
            n = len(cs)
            cs.append(send(chunk(yp, r), chunk(yp, r), gc_s.at[t, n], gc_r.at[t, n], sib))

        uc, dc, hu, hd, zc = [], [], [], [], []

        def around(r):
            uc.append(send(chunk(y, r), chunk(y, r), gy_s.at[t, 0, r], gy_r.at[t, 0, r], up))
            dc.append(send(chunk(y, r), chunk(y, r), gy_s.at[t, 1, r], gy_r.at[t, 1, r], dn))

        if t == 0:
            around(0)
        for r in (1, 2, 3):
            zc.append(send(chunk(y, 0), chunk(y, 0), gz_s.at[t, r - 1], gz_r.at[t, r - 1], (seq_of(y, zz[r], c), j)))
        to_sib(y, 0)
        yield
        if t == 1:
            around(0)
        for r in (1, 2, 3):
            zc[r - 1].wait_recv()
            around(r)
            to_sib(y, r)
        yield
        for r in range(4):
            uc[r].wait_recv()
            hu.append(send(half(yy[2], r, 0), half(yy[2], r, 0), gf_s.at[t, 0, r], gf_r.at[t, 0, r], up))
            to_sib(yy[2], r)
            dc[r].wait_recv()
            hd.append(send(half(yy[1], r, 1), half(yy[1], r, 1), gf_s.at[t, 1, r], gf_r.at[t, 1, r], dn))
            to_sib(yy[1], r)
            if r == 1:
                yield
        yield
        for r in range(4):
            hu[r].wait_recv()
            hd[r].wait_recv()
            to_sib(yy[0], r)
        yield
        for cp in cs:
            cp.wait_recv()

    def add(dst, a, b, *more):
        t = a.astype(f32) + b.astype(f32)
        for m in more:
            t = t + m.astype(f32)
        return t.astype(dst)

    def reduce(t, out_ref):
        mine = part.at[t, c]
        c0, cb, cz = [None] * 4, {}, [None] * 4
        for r in ORDER:
            collect(t, 1 - c, r)
            c0[r] = send(part.at[t, 1 - c, :, zz[r]], rx0.at[t, r], s0.at[t, r], r0.at[t, r], sib)
        for r in ORDER:
            collect(t, c, r)
        yield
        for r in ORDER:
            c0[r].wait_recv()
            for g in range(3):
                acc[t, g, r] = add(bf, mine[yy[g], zz[r]], rx0[t, r, yy[g]])
                cb[g, r] = send(acc.at[t, g, r], rxb.at[t, g, r], sb.at[t, g, r], rb.at[t, g, r], (seq_of(yy[g], z, c), j))
        yield
        for r in ORDER:
            for g in range(3):
                cb[g, r].wait_recv()
            if r:
                acc[t, 3, r] = add(bf, mine[y, zz[r]], rx0[t, r, y], rxb[t, 0, r], rxb[t, 1, r], rxb[t, 2, r])
                cz[r] = send(acc.at[t, 3, r], rxz.at[t, r - 1], sz.at[t, r - 1], rz.at[t, r - 1], (seq_of(y, zz[r], c), j))
                if r == 2:
                    yield
            else:
                zown[t] = add(f32, mine[y, z], rx0[t, 0, y], rxb[t, 0, 0], rxb[t, 1, 0], rxb[t, 2, 0])
        yield
        for r in (1, 2, 3):
            cz[r].wait_recv()
        for h in range(NK):
            p, sl = h // 4, slice((h % 4) * 32, (h % 4) * 32 + 32)
            res[t, h] = add(bf, zown[t, p, sl, :], rxz[t, 0, p, sl, :], rxz[t, 1, p, sl, :], rxz[t, 2, p, sl, :])
        ch = []
        for d in range(1, NK):
            h = (j + d) % NK
            ch.append(send(res.at[t, h], rxh.at[t, NK - d], sh.at[t, d - 1], rh.at[t, d - 1], (i, h)))
        yield
        for d in range(NK):
            col = pl.ds(pl.multiple_of(((j + d) % NK) * H, H), H)
            if d == 0:
                out_ref[:, col] = res[t, j]
            else:
                ch[NK - d - 1].wait_recv()
                out_ref[:, col] = rxh[t, d]

    def advance(flow, n=1):
        for _ in range(n):
            next(flow, None)

    def prepare(b):
        for g in range(G):
            qb = q_ref[b * B:(b + 1) * B, g * H:(g + 1) * H]
            ob = do_ref[b * B:(b + 1) * B, g * H:(g + 1) * H]
            qr[b, g * B:(g + 1) * B, :] = qb
            dor[b, g * B:(g + 1) * B, :] = ob
            qT[b, :, g * B:(g + 1) * B] = qb.T
            doT[b, :, g * B:(g + 1) * B] = ob.T

    def two(t, b, n):
        got = []
        for p in range(2):
            got.append(kva[t][tab[2 * n + p, b]])
        return jnp.concatenate(got, 0)

    def loop(lo, hi, fn, unroll=UNROLL):
        def body(n, _):
            fn(n)
            return 0
        lax.fori_loop(lo, hi, body, 0, unroll=unroll)

    def scores(b, lo, hi):
        def one(n, first=False):
            s = jnp.dot(two(0, b, n), qT[b], preferred_element_type=f32)
            for p in range(2):
                x = jnp.exp2(s[p * B:(p + 1) * B] * C2)
                if first and p == 0:
                    key = lax.broadcasted_iota(jnp.int32, (B, R), 0)
                    qry = lax.broadcasted_iota(jnp.int32, (B, R), 1) % B
                    x = jnp.where(key <= qry, x, 0.0)
                e_buf[b, n, p * B:(p + 1) * B, :] = x
                t = jnp.sum(x.reshape(B // 8, 8, R), 0) * tab[2 * n + p, 2 + b].astype(f32)
                if first and p == 0:
                    racc[b] = t
                else:
                    racc[b] += t
        if lo == 0:
            one(0, True)
            lo = 1
        loop(lo, hi, one)
        if hi == NP:
            rinv[b] = jnp.broadcast_to(1.0 / jnp.sum(racc[b], 0, keepdims=True), (8, R))

    def weights(b, n):
        return jnp.concatenate([e_buf[b, n, p * B:(p + 1) * B, :] * (rinv[b, 0:1, :] * tab[2 * n + p, 2 + b].astype(f32)) for p in range(2)], 0)

    def values(b, lo, hi):
        def one(n):
            w = weights(b, n)
            e_buf[b, n] = w
            o = jnp.dot(w.astype(bf), dor[b], preferred_element_type=f32)
            for p in range(2):
                pair_buf[b * NB + 2 * n + p] = o[p * B:(p + 1) * B]
        loop(lo, hi, one)

    def products(b, lo, hi):
        def one(n):
            p = jnp.dot(two(1, b, n), doT[b], preferred_element_type=f32)
            p_buf[n] = p
            racc[b] += jnp.sum((e_buf[b, n] * p).reshape(2 * B // 8, 8, R), 0)
        if lo == 0:
            racc[b] = jnp.zeros((8, R), f32)
        loop(lo, hi, one)
        if hi == NP:
            delta[b] = jnp.broadcast_to(jnp.sum(racc[b], 0, keepdims=True), (8, R))

    def grads(b, lo, hi):
        def one(n):
            ds = (e_buf[b, n] * (p_buf[n] - delta[b, 0:1, :])).astype(bf)
            o = jnp.dot(ds, qr[b], preferred_element_type=f32)
            for p in range(2):
                pair_buf[b * NB + 2 * n + p] = o[p * B:(p + 1) * B]
            e_buf[b, n] = ds.astype(f32)
        loop(lo, hi, one)

    def queries(b, lo, hi):
        def one(n):
            dqT[...] += lax.dot_general(two(0, b, n), e_buf[b, n].astype(bf), (((0,), (0,)), ((), ())), preferred_element_type=f32)
        if lo == 0:
            dqT[...] = jnp.zeros_like(dqT)
        loop(lo, hi, one)
        if hi == NP:
            for g in range(G):
                dq_ref[b * B:(b + 1) * B, g * H:(g + 1) * H] = (dqT[:, g * B:(g + 1) * B].T * SC).astype(bf)

    def collect(t, core, r):
        def one(m):
            yp, p = m // 2, m % 2
            k = 2 * seq_of(yp, zz[r], core) + p
            v = pair_buf[tab[NB, k]] + pair_buf[tab[NB + 1, k]]
            part[t, core, yp, zz[r], p] = (v if t else v * SC).astype(bf)
        loop(0, 8, one, 4)

    pair_buf[2 * NB] = jnp.zeros((B, H), f32)
    loads[2].wait()
    loads[3].wait()
    prepare(0)
    for cp in heads:
        cp.wait_recv()
    kf, vf = gather(0), gather(1)
    advance(kf)
    prepare(1)
    for cp in loads[4:]:
        cp.wait()
    lane = lax.broadcasted_iota(jnp.int32, (NB, NBLK), 1)
    entry = lax.broadcasted_iota(jnp.int32, (NB, NBLK), 0)
    wide = lax.broadcasted_iota(jnp.int32, (NB, H), 1)
    mixed = jnp.zeros((NB, H), jnp.int32)
    for b in range(2):
        pos = span[2 * i + b]
        col = jnp.sum(jnp.where(lane == pos, lists[...], 0), 1, keepdims=True)
        hit = row[...] == col
        mixed = jnp.where(wide == b, jnp.min(jnp.where(hit, lane, NBLK - 1), 1, keepdims=True), mixed)
        valid = entry < counts[pos]
        mixed = jnp.where(jnp.logical_and(wide == 2 + b, lax.broadcasted_iota(jnp.int32, (NB, H), 0) < counts[pos]), 1, mixed)
        at = jnp.where(jnp.logical_and(hit, valid), entry + b * NB, 2 * NB)
        tab_v[NB + b:NB + b + 1, 0:NBLK] = jnp.min(at, 0, keepdims=True)
    tab_v[0:NB, :] = mixed
    to_scalar = pltpu.make_async_copy(tab_v, tab, s_in.at[8])
    to_scalar.start()
    to_scalar.wait()
    advance(kf)
    advance(vf)
    advance(kf, 2)
    advance(vf)
    advance(kf, 2)
    scores(0, 0, NP)
    advance(vf)
    values(0, 0, NP)
    advance(vf)
    scores(1, 0, NP)
    advance(vf)
    values(1, 0, NP)
    vr = reduce(1, vo_ref)
    advance(vr)
    advance(vf)
    products(0, 0, NP)
    advance(vr)
    grads(0, 0, NP)
    products(1, 0, NP)
    grads(1, 0, NP)
    kr = reduce(0, ko_ref)
    advance(kr)
    advance(vr)
    queries(0, 0, NP)
    advance(kr)
    advance(vr)
    queries(1, 0, NP)
    advance(vr)
    advance(kr, 2)
    advance(vr)
    for _ in kr:
        pass
    for _ in vr:
        pass
    for cp in sends:
        cp.wait_send()


def finish_kernel(a, b, c, ao, bo, co):
    ao[...] = a[...]
    bo[...] = b[...]
    co[...] = c[...]


def finish(*outs):
    return pl.pallas_call(finish_kernel, out_shape=tuple(jax.ShapeDtypeStruct(o.shape, o.dtype) for o in outs))(*outs)


def fused(lists, counts, span, row, k, v, q, do):
    vm = pl.BlockSpec(memory_space=pltpu.VMEM)
    hb = pl.BlockSpec(memory_space=pl.ANY)
    V = pltpu.VMEM
    D = pltpu.SemaphoreType.DMA
    tok = jax.ShapeDtypeStruct((32, NK * H), bf)
    return pl.pallas_call(
        kernel,
        out_shape=(jax.ShapeDtypeStruct((2 * B, R), bf), tok, tok),
        in_specs=[hb] * 8,
        out_specs=[vm] * 3,
        scratch_shapes=[
            V((NB, NBLK), jnp.int32), pltpu.SMEM((NBLK,), jnp.int32), pltpu.SMEM((NBLK,), jnp.int32), V((1, NBLK), jnp.int32),
            V((NB + 8, H), jnp.int32), pltpu.SMEM((NB + 8, H), jnp.int32),
            V((32, NK * H), bf), V((32, NK * H), bf), V((2 * B, R), bf), V((2 * B, R), bf),
            V((NK, 2, 32, H), bf), V((NBLK, B, H), bf), V((NBLK, B, H), bf), V((2, 2, 4, 4, 2, B, H), bf),
            V((2, H, R), bf), V((2, H, R), bf), V((2, R, H), bf), V((2, R, H), bf),
            V((2, NP, 2 * B, R), f32), V((NP, 2 * B, R), f32), V((2 * NB + 1, B, H), f32), V((H, R), f32),
            V((2, 8, R), f32), V((2, 8, R), f32), V((2, 8, R), f32),
            V((2, 4, 4, 2, B, H), bf), V((2, 4, 4, 2, B, H), bf), V((2, 3, 4, 2, B, H), bf),
            V((2, 3, 2, B, H), bf), V((2, 2, B, H), f32), V((2, NK, 32, H), bf), V((2, NK, 32, H), bf),
            D((9,)), D((2, 7)), D((2, 7)), D((2, 3)), D((2, 3)), D((2, 2, 4)), D((2, 2, 4)), D((2, 2, 4)), D((2, 2, 4)), D((2, 16)), D((2, 16)),
            D((2, 4)), D((2, 4)), D((2, 3, 4)), D((2, 3, 4)), D((2, 3)), D((2, 3)), D((2, 7)), D((2, 7)),
        ],
        compiler_params=pltpu.CompilerParams(collective_id=0, has_side_effects=True, vmem_limit_bytes=62 << 20),
    )(lists, counts, span, row, k, v, q, do)


def shards(queries, key_vector_rows, value_vector_rows, output_gradient, key_lists, block_counts, span_table):
    return finish(*fused(key_lists.T, block_counts, span_table, span_table.reshape(1, NBLK), key_vector_rows, value_vector_rows, queries, output_gradient))


def solution(mesh):
    tokens = P(("seq", "kvh"), None)
    heads = P("seq", "kvh")
    return jax.shard_map(
        shards,
        mesh=mesh,
        in_specs=(heads, tokens, tokens, heads, P(), P(), P()),
        out_specs=(heads, tokens, tokens),
        check_vma=False,
    )
```

```python
import jax
import jax.numpy as jnp
from jax import lax
from jax.experimental import pallas as pl
from jax.experimental.pallas import tpu as pltpu
from jax.sharding import PartitionSpec as P
H = 128
G = 8
B = 128
NB = 24
NP = NB // 2
NBLK = 64
NK = 8
SC = H ** -0.5
C2 = SC * 1.4426950408889634
R = G * B
bf = jnp.bfloat16
f32 = jnp.float32
MESH = pl.DeviceIdType.MESH
UNROLL = 6


def place():
    i = lax.axis_index("seq")
    j = lax.axis_index("kvh")
    return i, j, i // 8, (i // 2) % 4, i % 2


def seq_of(y, z, c):
    return (y * 4 + z) * 2 + c


def zrel(z):
    return [z, z + 1 - 2 * (z % 2), (z + 2) % 4, 3 - z]


ORDER = (1, 2, 3, 0)


def kernel(lists_hbm, counts_hbm, span_hbm, row_hbm, k_hbm, v_hbm, q_hbm, do_hbm, dq_hbm, ko_ref, vo_ref,
           lists, counts, span, row, tab_v, tab, kin, vin, dq_ref, q_ref, do_ref, tx, ka, va, part, qT, doT, qr, dor, e_buf, p_buf, pair_buf, dqT, racc, rinv, delta,
           rx0, acc, rxb, rxz, zown, res, rxh,
           s_in, hs, hr, gz_s, gz_r, gy_s, gy_r, gf_s, gf_r, gc_s, gc_r,
           s0, r0, sb, rb, sz, rz, sh, rh):
    i, j, y, z, c = place()
    zz = zrel(z)
    yy = [(y + 2) % 4, (y + 1) % 4, (y + 3) % 4, y]
    sib = (seq_of(y, z, 1 - c), j)
    up = (seq_of(yy[1], z, c), j)
    dn = (seq_of(yy[2], z, c), j)
    kva = (ka, va)
    sends = []

    def send(src, dst, ss, rs, dev):
        cp = pltpu.make_async_remote_copy(src_ref=src, dst_ref=dst, send_sem=ss, recv_sem=rs, device_id=dev, device_id_type=MESH)
        cp.start()
        sends.append(cp)
        return cp

    barrier = pltpu.get_barrier_semaphore()
    near = [sib, up, dn, (seq_of(yy[0], z, c), j)] + [(seq_of(y, zz[r], c), j) for r in (1, 2, 3)]
    for dev in near + [(i, (j + d) % NK) for d in range(1, NK)]:
        pl.semaphore_signal(barrier, inc=1, device_id=dev, device_id_type=MESH)
    loads = [pltpu.make_async_copy(a, b, s_in.at[n]) for n, (a, b) in enumerate(((k_hbm, kin), (v_hbm, vin), (q_hbm, q_ref), (do_hbm, do_ref), (lists_hbm, lists), (counts_hbm, counts), (span_hbm, span), (row_hbm, row)))]
    for cp in loads:
        cp.start()
    loads[0].wait()
    loads[1].wait()
    for h in range(NK):
        tx[h, 0] = kin[:, h * H:(h + 1) * H]
        tx[h, 1] = vin[:, h * H:(h + 1) * H]
    pl.semaphore_wait(barrier, len(near) + NK - 1)
    rows = pl.ds(pl.multiple_of((j % 4) * 32, 32), 32)
    heads = []
    for t in range(2):
        for d in range(1, NK):
            h = (j + d) % NK
            heads.append(send(tx.at[h, t], kva[t].at[2 * i + j // 4, rows, :], hs.at[t, d - 1], hr.at[t, d - 1], (i, h)))
    for t in range(2):
        kva[t][2 * i + j // 4, rows, :] = tx[j, t]

    def gather(t):
        def chunk(yp, r):
            return kva[t].at[pl.ds(2 * seq_of(yp, zz[r], c), 2)]

        def half(yp, r, p):
            return kva[t].at[2 * seq_of(yp, zz[r], c) + p]

        cs = []

        def to_sib(yp, r):
            n = len(cs)
            cs.append(send(chunk(yp, r), chunk(yp, r), gc_s.at[t, n], gc_r.at[t, n], sib))

        uc, dc, hu, hd, zc = [], [], [], [], []

        def around(r):
            uc.append(send(chunk(y, r), chunk(y, r), gy_s.at[t, 0, r], gy_r.at[t, 0, r], up))
            dc.append(send(chunk(y, r), chunk(y, r), gy_s.at[t, 1, r], gy_r.at[t, 1, r], dn))

        if t == 0:
            around(0)
        for r in (1, 2, 3):
            zc.append(send(chunk(y, 0), chunk(y, 0), gz_s.at[t, r - 1], gz_r.at[t, r - 1], (seq_of(y, zz[r], c), j)))
        to_sib(y, 0)
        yield
        if t == 1:
            around(0)
        for r in (1, 2, 3):
            zc[r - 1].wait_recv()
            around(r)
            to_sib(y, r)
        yield
        for r in range(4):
            uc[r].wait_recv()
            hu.append(send(half(yy[2], r, 0), half(yy[2], r, 0), gf_s.at[t, 0, r], gf_r.at[t, 0, r], up))
            to_sib(yy[2], r)
            dc[r].wait_recv()
            hd.append(send(half(yy[1], r, 1), half(yy[1], r, 1), gf_s.at[t, 1, r], gf_r.at[t, 1, r], dn))
            to_sib(yy[1], r)
            if r == 1:
                yield
        yield
        for r in range(4):
            hu[r].wait_recv()
            hd[r].wait_recv()
            to_sib(yy[0], r)
        yield
        for cp in cs:
            cp.wait_recv()

    def add(dst, a, b, *more):
        t = a.astype(f32) + b.astype(f32)
        for m in more:
            t = t + m.astype(f32)
        return t.astype(dst)

    def reduce(t, out_ref):
        mine = part.at[t, c]
        c0, cb, cz = [None] * 4, {}, [None] * 4
        for r in ORDER:
            collect(t, 1 - c, r)
            c0[r] = send(part.at[t, 1 - c, :, zz[r]], rx0.at[t, r], s0.at[t, r], r0.at[t, r], sib)
        for r in ORDER:
            collect(t, c, r)
        yield
        for r in ORDER:
            c0[r].wait_recv()
            for g in range(3):
                acc[t, g, r] = add(bf, mine[yy[g], zz[r]], rx0[t, r, yy[g]])
                cb[g, r] = send(acc.at[t, g, r], rxb.at[t, g, r], sb.at[t, g, r], rb.at[t, g, r], (seq_of(yy[g], z, c), j))
        yield
        for r in ORDER:
            for g in range(3):
                cb[g, r].wait_recv()
            if r:
                acc[t, 3, r] = add(bf, mine[y, zz[r]], rx0[t, r, y], rxb[t, 0, r], rxb[t, 1, r], rxb[t, 2, r])
                cz[r] = send(acc.at[t, 3, r], rxz.at[t, r - 1], sz.at[t, r - 1], rz.at[t, r - 1], (seq_of(y, zz[r], c), j))
                if r == 2:
                    yield
            else:
                zown[t] = add(f32, mine[y, z], rx0[t, 0, y], rxb[t, 0, 0], rxb[t, 1, 0], rxb[t, 2, 0])
        yield
        for r in (1, 2, 3):
            cz[r].wait_recv()
        for h in range(NK):
            p, sl = h // 4, slice((h % 4) * 32, (h % 4) * 32 + 32)
            res[t, h] = add(bf, zown[t, p, sl, :], rxz[t, 0, p, sl, :], rxz[t, 1, p, sl, :], rxz[t, 2, p, sl, :])
        ch = []
        for d in range(1, NK):
            h = (j + d) % NK
            ch.append(send(res.at[t, h], rxh.at[t, NK - d], sh.at[t, d - 1], rh.at[t, d - 1], (i, h)))
        yield
        for d in range(NK):
            col = pl.ds(pl.multiple_of(((j + d) % NK) * H, H), H)
            if d == 0:
                out_ref[:, col] = res[t, j]
            else:
                ch[NK - d - 1].wait_recv()
                out_ref[:, col] = rxh[t, d]

    def advance(flow, n=1):
        for _ in range(n):
            next(flow, None)

    def prepare(b):
        for g in range(G):
            qb = q_ref[b * B:(b + 1) * B, g * H:(g + 1) * H]
            ob = do_ref[b * B:(b + 1) * B, g * H:(g + 1) * H]
            qr[b, g * B:(g + 1) * B, :] = qb
            dor[b, g * B:(g + 1) * B, :] = ob
            qT[b, :, g * B:(g + 1) * B] = qb.T
            doT[b, :, g * B:(g + 1) * B] = ob.T

    def two(t, b, n):
        got = []
        for p in range(2):
            got.append(kva[t][tab[2 * n + p, b]])
        return jnp.concatenate(got, 0)

    def loop(lo, hi, fn, unroll=UNROLL):
        def body(n, _):
            fn(n)
            return 0
        lax.fori_loop(lo, hi, body, 0, unroll=unroll)

    def scores(b, lo, hi):
        def one(n, first=False):
            s = jnp.dot(two(0, b, n), qT[b], preferred_element_type=f32)
            for p in range(2):
                x = jnp.exp2(s[p * B:(p + 1) * B] * C2)
                if first and p == 0:
                    key = lax.broadcasted_iota(jnp.int32, (B, R), 0)
                    qry = lax.broadcasted_iota(jnp.int32, (B, R), 1) % B
                    x = jnp.where(key <= qry, x, 0.0)
                e_buf[b, n, p * B:(p + 1) * B, :] = x
                t = jnp.sum(x.reshape(B // 8, 8, R), 0) * tab[2 * n + p, 2 + b].astype(f32)
                if first and p == 0:
                    racc[b] = t
                else:
                    racc[b] += t
        if lo == 0:
            one(0, True)
            lo = 1
        loop(lo, hi, one)
        if hi == NP:
            rinv[b] = jnp.broadcast_to(1.0 / jnp.sum(racc[b], 0, keepdims=True), (8, R))

    def weights(b, n):
        return jnp.concatenate([e_buf[b, n, p * B:(p + 1) * B, :] * (rinv[b, 0:1, :] * tab[2 * n + p, 2 + b].astype(f32)) for p in range(2)], 0)

    def values(b, lo, hi):
        def one(n):
            w = weights(b, n)
            e_buf[b, n] = w
            o = jnp.dot(w.astype(bf), dor[b], preferred_element_type=f32)
            for p in range(2):
                pair_buf[b * NB + 2 * n + p] = o[p * B:(p + 1) * B]
        loop(lo, hi, one)

    def products(b, lo, hi):
        def one(n):
            p = jnp.dot(two(1, b, n), doT[b], preferred_element_type=f32)
            p_buf[n] = p
            racc[b] += jnp.sum((e_buf[b, n] * p).reshape(2 * B // 8, 8, R), 0)
        if lo == 0:
            racc[b] = jnp.zeros((8, R), f32)
        loop(lo, hi, one)
        if hi == NP:
            delta[b] = jnp.broadcast_to(jnp.sum(racc[b], 0, keepdims=True), (8, R))

    def grads(b, lo, hi):
        def one(n):
            ds = (e_buf[b, n] * (p_buf[n] - delta[b, 0:1, :])).astype(bf)
            o = jnp.dot(ds, qr[b], preferred_element_type=f32)
            for p in range(2):
                pair_buf[b * NB + 2 * n + p] = o[p * B:(p + 1) * B]
            e_buf[b, n] = ds.astype(f32)
        loop(lo, hi, one)

    def queries(b, lo, hi):
        def one(n):
            dqT[...] += lax.dot_general(two(0, b, n), e_buf[b, n].astype(bf), (((0,), (0,)), ((), ())), preferred_element_type=f32)
        if lo == 0:
            dqT[...] = jnp.zeros_like(dqT)
        loop(lo, hi, one)
        if hi == NP:
            for g in range(G):
                dq_ref[b * B:(b + 1) * B, g * H:(g + 1) * H] = (dqT[:, g * B:(g + 1) * B].T * SC).astype(bf)

    def collect(t, core, r):
        def one(m):
            yp, p = m // 2, m % 2
            k = 2 * seq_of(yp, zz[r], core) + p
            v = pair_buf[tab[NB, k]] + pair_buf[tab[NB + 1, k]]
            part[t, core, yp, zz[r], p] = (v if t else v * SC).astype(bf)
        loop(0, 8, one, 4)

    pair_buf[2 * NB] = jnp.zeros((B, H), f32)
    loads[2].wait()
    loads[3].wait()
    prepare(0)
    for cp in heads[:NK - 1]:
        cp.wait_recv()
    kf, vf = gather(0), gather(1)
    advance(kf)
    prepare(1)
    for cp in loads[4:]:
        cp.wait()
    lane = lax.broadcasted_iota(jnp.int32, (NB, NBLK), 1)
    entry = lax.broadcasted_iota(jnp.int32, (NB, NBLK), 0)
    wide = lax.broadcasted_iota(jnp.int32, (NB, H), 1)
    mixed = jnp.zeros((NB, H), jnp.int32)
    for b in range(2):
        pos = span[2 * i + b]
        col = jnp.sum(jnp.where(lane == pos, lists[...], 0), 1, keepdims=True)
        hit = row[...] == col
        mixed = jnp.where(wide == b, jnp.min(jnp.where(hit, lane, NBLK - 1), 1, keepdims=True), mixed)
        valid = entry < counts[pos]
        mixed = jnp.where(jnp.logical_and(wide == 2 + b, lax.broadcasted_iota(jnp.int32, (NB, H), 0) < counts[pos]), 1, mixed)
        at = jnp.where(jnp.logical_and(hit, valid), entry + b * NB, 2 * NB)
        tab_v[NB + b:NB + b + 1, 0:NBLK] = jnp.min(at, 0, keepdims=True)
    tab_v[0:NB, :] = mixed
    to_scalar = pltpu.make_async_copy(tab_v, tab, s_in.at[8])
    to_scalar.start()
    to_scalar.wait()
    advance(kf)
    for cp in heads[NK - 1:]:
        cp.wait_recv()
    advance(vf)
    advance(kf, 2)
    advance(vf)
    advance(kf, 2)
    scores(0, 0, NP)
    advance(vf)
    values(0, 0, NP)
    advance(vf)
    scores(1, 0, NP)
    advance(vf)
    values(1, 0, NP)
    vr = reduce(1, vo_ref)
    advance(vr)
    advance(vf)
    products(0, 0, NP)
    advance(vr)
    grads(0, 0, NP)
    products(1, 0, NP)
    grads(1, 0, NP)
    kr = reduce(0, ko_ref)
    advance(kr)
    advance(vr)
    queries(0, 0, NP)
    advance(kr)
    advance(vr)
    queries(1, 0, NP)
    leave = pltpu.make_async_copy(dq_ref, dq_hbm, s_in.at[9])
    leave.start()
    advance(vr)
    advance(kr, 2)
    advance(vr)
    for _ in kr:
        pass
    for _ in vr:
        pass
    leave.wait()
    for cp in sends:
        cp.wait_send()


def finish_kernel(a, b, c, ao, bo, co):
    ao[...] = a[...]
    bo[...] = b[...]
    co[...] = c[...]


def finish(*outs):
    return pl.pallas_call(finish_kernel, out_shape=tuple(jax.ShapeDtypeStruct(o.shape, o.dtype) for o in outs))(*outs)


def fused(lists, counts, span, row, k, v, q, do):
    vm = pl.BlockSpec(memory_space=pltpu.VMEM)
    hb = pl.BlockSpec(memory_space=pl.ANY)
    V = pltpu.VMEM
    D = pltpu.SemaphoreType.DMA
    tok = jax.ShapeDtypeStruct((32, NK * H), bf)
    return pl.pallas_call(
        kernel,
        out_shape=(jax.ShapeDtypeStruct((2 * B, R), bf), tok, tok),
        in_specs=[hb] * 8,
        out_specs=[hb, vm, vm],
        scratch_shapes=[
            V((NB, NBLK), jnp.int32), pltpu.SMEM((NBLK,), jnp.int32), pltpu.SMEM((NBLK,), jnp.int32), V((1, NBLK), jnp.int32),
            V((NB + 8, H), jnp.int32), pltpu.SMEM((NB + 8, H), jnp.int32),
            V((32, NK * H), bf), V((32, NK * H), bf), V((2 * B, R), bf), V((2 * B, R), bf), V((2 * B, R), bf),
            V((NK, 2, 32, H), bf), V((NBLK, B, H), bf), V((NBLK, B, H), bf), V((2, 2, 4, 4, 2, B, H), bf),
            V((2, H, R), bf), V((2, H, R), bf), V((2, R, H), bf), V((2, R, H), bf),
            V((2, NP, 2 * B, R), f32), V((NP, 2 * B, R), f32), V((2 * NB + 1, B, H), f32), V((H, R), f32),
            V((2, 8, R), f32), V((2, 8, R), f32), V((2, 8, R), f32),
            V((2, 4, 4, 2, B, H), bf), V((2, 4, 4, 2, B, H), bf), V((2, 3, 4, 2, B, H), bf),
            V((2, 3, 2, B, H), bf), V((2, 2, B, H), f32), V((2, NK, 32, H), bf), V((2, NK, 32, H), bf),
            D((10,)), D((2, 7)), D((2, 7)), D((2, 3)), D((2, 3)), D((2, 2, 4)), D((2, 2, 4)), D((2, 2, 4)), D((2, 2, 4)), D((2, 16)), D((2, 16)),
            D((2, 4)), D((2, 4)), D((2, 3, 4)), D((2, 3, 4)), D((2, 3)), D((2, 3)), D((2, 7)), D((2, 7)),
        ],
        compiler_params=pltpu.CompilerParams(collective_id=0, has_side_effects=True, vmem_limit_bytes=62 << 20),
    )(lists, counts, span, row, k, v, q, do)


def shards(queries, key_vector_rows, value_vector_rows, output_gradient, key_lists, block_counts, span_table):
    return finish(*fused(key_lists.T, block_counts, span_table, span_table.reshape(1, NBLK), key_vector_rows, value_vector_rows, queries, output_gradient))


def solution(mesh):
    tokens = P(("seq", "kvh"), None)
    heads = P("seq", "kvh")
    return jax.shard_map(
        shards,
        mesh=mesh,
        in_specs=(heads, tokens, tokens, heads, P(), P(), P()),
        out_specs=(heads, tokens, tokens),
        check_vma=False,
    )
```

```python
import jax
import jax.numpy as jnp
from jax import lax
from jax.experimental import pallas as pl
from jax.experimental.pallas import tpu as pltpu
from jax.sharding import PartitionSpec as P
H = 128
G = 8
B = 128
NB = 24
NP = NB // 2
NBLK = 64
NK = 8
SC = H ** -0.5
C2 = SC * 1.4426950408889634
R = G * B
bf = jnp.bfloat16
f32 = jnp.float32
MESH = pl.DeviceIdType.MESH
UNROLL = 6


def place():
    i = lax.axis_index("seq")
    j = lax.axis_index("kvh")
    return i, j, i // 8, (i // 2) % 4, i % 2


def seq_of(y, z, c):
    return (y * 4 + z) * 2 + c


def zrel(z):
    return [z, z + 1 - 2 * (z % 2), (z + 2) % 4, 3 - z]


ORDER = (1, 2, 3, 0)


def kernel(lists_hbm, counts_hbm, span_hbm, row_hbm, k_hbm, v_hbm, q_hbm, do_hbm, dq_hbm, ko_ref, vo_ref,
           lists, counts, span, row, tab_v, tab, kin, vin, dq_ref, q_ref, do_ref, tx, ka, va, part, qT, doT, qr, dor, e_buf, p_buf, pair_buf, dqT, racc, rinv, delta,
           rx0, acc, rxb, rxz, zown, res, rxh,
           s_in, hs, hr, gz_s, gz_r, gy_s, gy_r, gf_s, gf_r, gc_s, gc_r,
           s0, r0, sb, rb, sz, rz, sh, rh):
    i, j, y, z, c = place()
    zz = zrel(z)
    yy = [(y + 2) % 4, (y + 1) % 4, (y + 3) % 4, y]
    sib = (seq_of(y, z, 1 - c), j)
    up = (seq_of(yy[1], z, c), j)
    dn = (seq_of(yy[2], z, c), j)
    kva = (ka, va)
    sends = []

    def send(src, dst, ss, rs, dev):
        cp = pltpu.make_async_remote_copy(src_ref=src, dst_ref=dst, send_sem=ss, recv_sem=rs, device_id=dev, device_id_type=MESH)
        cp.start()
        sends.append(cp)
        return cp

    barrier = pltpu.get_barrier_semaphore()
    near = [sib, up, dn, (seq_of(yy[0], z, c), j)] + [(seq_of(y, zz[r], c), j) for r in (1, 2, 3)]
    for dev in near + [(i, (j + d) % NK) for d in range(1, NK)]:
        pl.semaphore_signal(barrier, inc=1, device_id=dev, device_id_type=MESH)
    loads = [pltpu.make_async_copy(a, b, s_in.at[n]) for n, (a, b) in enumerate(((k_hbm, kin), (v_hbm, vin), (q_hbm, q_ref), (do_hbm, do_ref), (lists_hbm, lists), (counts_hbm, counts), (span_hbm, span), (row_hbm, row)))]
    for cp in loads:
        cp.start()
    loads[0].wait()
    loads[1].wait()
    for h in range(NK):
        tx[h, 0] = kin[:, h * H:(h + 1) * H]
        tx[h, 1] = vin[:, h * H:(h + 1) * H]
    pl.semaphore_wait(barrier, len(near) + NK - 1)
    rows = pl.ds(pl.multiple_of((j % 4) * 32, 32), 32)
    heads = []
    for t in range(2):
        for d in range(1, NK):
            h = (j + d) % NK
            heads.append(send(tx.at[h, t], kva[t].at[2 * i + j // 4, rows, :], hs.at[t, d - 1], hr.at[t, d - 1], (i, h)))
    for t in range(2):
        kva[t][2 * i + j // 4, rows, :] = tx[j, t]

    def gather(t):
        def chunk(yp, r):
            return kva[t].at[pl.ds(2 * seq_of(yp, zz[r], c), 2)]

        def half(yp, r, p):
            return kva[t].at[2 * seq_of(yp, zz[r], c) + p]

        cs = []

        def to_sib(yp, r):
            n = len(cs)
            cs.append(send(chunk(yp, r), chunk(yp, r), gc_s.at[t, n], gc_r.at[t, n], sib))

        uc, dc, hu, hd, zc = [], [], [], [], []

        def around(r):
            uc.append(send(chunk(y, r), chunk(y, r), gy_s.at[t, 0, r], gy_r.at[t, 0, r], up))
            dc.append(send(chunk(y, r), chunk(y, r), gy_s.at[t, 1, r], gy_r.at[t, 1, r], dn))

        if t == 0:
            around(0)
        for r in (1, 2, 3):
            zc.append(send(chunk(y, 0), chunk(y, 0), gz_s.at[t, r - 1], gz_r.at[t, r - 1], (seq_of(y, zz[r], c), j)))
        to_sib(y, 0)
        yield
        if t == 1:
            around(0)
        for r in (1, 2, 3):
            zc[r - 1].wait_recv()
            around(r)
            to_sib(y, r)
        yield
        for r in range(4):
            uc[r].wait_recv()
            hu.append(send(half(yy[2], r, 0), half(yy[2], r, 0), gf_s.at[t, 0, r], gf_r.at[t, 0, r], up))
            to_sib(yy[2], r)
            dc[r].wait_recv()
            hd.append(send(half(yy[1], r, 1), half(yy[1], r, 1), gf_s.at[t, 1, r], gf_r.at[t, 1, r], dn))
            to_sib(yy[1], r)
            if r == 1:
                yield
        yield
        for r in range(4):
            hu[r].wait_recv()
            hd[r].wait_recv()
            to_sib(yy[0], r)
        yield
        for cp in cs:
            cp.wait_recv()

    def add(dst, a, b, *more):
        t = a.astype(f32) + b.astype(f32)
        for m in more:
            t = t + m.astype(f32)
        return t.astype(dst)

    def reduce(t, out_ref):
        mine = part.at[t, c]
        c0, cb, cz = [None] * 4, {}, [None] * 4
        for r in ORDER:
            collect(t, 1 - c, r)
            c0[r] = send(part.at[t, 1 - c, :, zz[r]], rx0.at[t, r], s0.at[t, r], r0.at[t, r], sib)
        for r in ORDER:
            collect(t, c, r)
        yield
        for r in ORDER:
            c0[r].wait_recv()
            for g in range(3):
                acc[t, g, r] = add(bf, mine[yy[g], zz[r]], rx0[t, r, yy[g]])
                cb[g, r] = send(acc.at[t, g, r], rxb.at[t, g, r], sb.at[t, g, r], rb.at[t, g, r], (seq_of(yy[g], z, c), j))
        yield
        for r in ORDER:
            for g in range(3):
                cb[g, r].wait_recv()
            if r:
                acc[t, 3, r] = add(bf, mine[y, zz[r]], rx0[t, r, y], rxb[t, 0, r], rxb[t, 1, r], rxb[t, 2, r])
                cz[r] = send(acc.at[t, 3, r], rxz.at[t, r - 1], sz.at[t, r - 1], rz.at[t, r - 1], (seq_of(y, zz[r], c), j))
                if r == 2:
                    yield
            else:
                zown[t] = add(f32, mine[y, z], rx0[t, 0, y], rxb[t, 0, 0], rxb[t, 1, 0], rxb[t, 2, 0])
        yield
        for r in (1, 2, 3):
            cz[r].wait_recv()
        for h in range(NK):
            p, sl = h // 4, slice((h % 4) * 32, (h % 4) * 32 + 32)
            res[t, h] = add(bf, zown[t, p, sl, :], rxz[t, 0, p, sl, :], rxz[t, 1, p, sl, :], rxz[t, 2, p, sl, :])
        ch = []
        for d in range(1, NK):
            h = (j + d) % NK
            ch.append(send(res.at[t, h], rxh.at[t, NK - d], sh.at[t, d - 1], rh.at[t, d - 1], (i, h)))
        yield
        for d in range(NK):
            col = pl.ds(pl.multiple_of(((j + d) % NK) * H, H), H)
            if d == 0:
                out_ref[:, col] = res[t, j]
            else:
                ch[NK - d - 1].wait_recv()
                out_ref[:, col] = rxh[t, d]

    def advance(flow, n=1):
        for _ in range(n):
            next(flow, None)

    def prepare(b):
        for g in range(G):
            qb = q_ref[b * B:(b + 1) * B, g * H:(g + 1) * H]
            ob = do_ref[b * B:(b + 1) * B, g * H:(g + 1) * H]
            qr[b, g * B:(g + 1) * B, :] = qb
            dor[b, g * B:(g + 1) * B, :] = ob
            qT[b, :, g * B:(g + 1) * B] = qb.T
            doT[b, :, g * B:(g + 1) * B] = ob.T

    def two(t, b, n):
        got = []
        for p in range(2):
            got.append(kva[t][tab[2 * n + p, b]])
        return jnp.concatenate(got, 0)

    def loop(lo, hi, fn, unroll=UNROLL):
        def body(n, _):
            fn(n)
            return 0
        lax.fori_loop(lo, hi, body, 0, unroll=unroll)

    def scores(b, lo, hi):
        def one(n, first=False):
            s = jnp.dot(two(0, b, n), qT[b], preferred_element_type=f32)
            for p in range(2):
                x = jnp.exp2(s[p * B:(p + 1) * B] * C2)
                if first and p == 0:
                    key = lax.broadcasted_iota(jnp.int32, (B, R), 0)
                    qry = lax.broadcasted_iota(jnp.int32, (B, R), 1) % B
                    x = jnp.where(key <= qry, x, 0.0)
                e_buf[b, n, p * B:(p + 1) * B, :] = x
                t = jnp.sum(x.reshape(B // 8, 8, R), 0) * tab[2 * n + p, 2 + b].astype(f32)
                if first and p == 0:
                    racc[b] = t
                else:
                    racc[b] += t
        if lo == 0:
            one(0, True)
            lo = 1
        loop(lo, hi, one)
        if hi == NP:
            rinv[b] = jnp.broadcast_to(1.0 / jnp.sum(racc[b], 0, keepdims=True), (8, R))

    def weights(b, n):
        return jnp.concatenate([e_buf[b, n, p * B:(p + 1) * B, :] * (rinv[b, 0:1, :] * tab[2 * n + p, 2 + b].astype(f32)) for p in range(2)], 0)

    def values(b, lo, hi):
        def one(n):
            w = weights(b, n)
            e_buf[b, n] = w
            o = jnp.dot(w.astype(bf), dor[b], preferred_element_type=f32)
            for p in range(2):
                pair_buf[b * NB + 2 * n + p] = o[p * B:(p + 1) * B]
        loop(lo, hi, one)

    def products(b, lo, hi):
        def one(n):
            p = jnp.dot(two(1, b, n), doT[b], preferred_element_type=f32)
            p_buf[n] = p
            racc[b] += jnp.sum((e_buf[b, n] * p).reshape(2 * B // 8, 8, R), 0)
        if lo == 0:
            racc[b] = jnp.zeros((8, R), f32)
        loop(lo, hi, one)
        if hi == NP:
            delta[b] = jnp.broadcast_to(jnp.sum(racc[b], 0, keepdims=True), (8, R))

    def grads(b, lo, hi):
        def one(n):
            ds = (e_buf[b, n] * (p_buf[n] - delta[b, 0:1, :])).astype(bf)
            o = jnp.dot(ds, qr[b], preferred_element_type=f32)
            for p in range(2):
                pair_buf[b * NB + 2 * n + p] = o[p * B:(p + 1) * B]
            e_buf[b, n] = ds.astype(f32)
        loop(lo, hi, one)

    def queries(b, lo, hi):
        def one(n):
            dqT[...] += lax.dot_general(two(0, b, n), e_buf[b, n].astype(bf), (((0,), (0,)), ((), ())), preferred_element_type=f32)
        if lo == 0:
            dqT[...] = jnp.zeros_like(dqT)
        loop(lo, hi, one)
        if hi == NP:
            for g in range(G):
                dq_ref[b * B:(b + 1) * B, g * H:(g + 1) * H] = (dqT[:, g * B:(g + 1) * B].T * SC).astype(bf)

    def collect(t, core, r):
        def one(m):
            yp, p = m // 2, m % 2
            k = 2 * seq_of(yp, zz[r], core) + p
            v = pair_buf[tab[NB, k]] + pair_buf[tab[NB + 1, k]]
            part[t, core, yp, zz[r], p] = (v if t else v * SC).astype(bf)
        loop(0, 8, one, 4)

    pair_buf[2 * NB] = jnp.zeros((B, H), f32)
    loads[2].wait()
    loads[3].wait()
    prepare(0)
    for cp in heads[:NK - 1]:
        cp.wait_recv()
    kf, vf = gather(0), gather(1)
    advance(kf)
    prepare(1)
    for cp in loads[4:]:
        cp.wait()
    lane = lax.broadcasted_iota(jnp.int32, (NB, NBLK), 1)
    entry = lax.broadcasted_iota(jnp.int32, (NB, NBLK), 0)
    wide = lax.broadcasted_iota(jnp.int32, (NB, H), 1)
    mixed = jnp.zeros((NB, H), jnp.int32)
    for b in range(2):
        pos = span[2 * i + b]
        col = jnp.sum(jnp.where(lane == pos, lists[...], 0), 1, keepdims=True)
        hit = row[...] == col
        mixed = jnp.where(wide == b, jnp.min(jnp.where(hit, lane, NBLK - 1), 1, keepdims=True), mixed)
        valid = entry < counts[pos]
        mixed = jnp.where(jnp.logical_and(wide == 2 + b, lax.broadcasted_iota(jnp.int32, (NB, H), 0) < counts[pos]), 1, mixed)
        at = jnp.where(jnp.logical_and(hit, valid), entry + b * NB, 2 * NB)
        tab_v[NB + b:NB + b + 1, 0:NBLK] = jnp.min(at, 0, keepdims=True)
    tab_v[0:NB, :] = mixed
    to_scalar = pltpu.make_async_copy(tab_v, tab, s_in.at[8])
    to_scalar.start()
    to_scalar.wait()
    advance(kf)
    for cp in heads[NK - 1:]:
        cp.wait_recv()
    advance(vf)
    advance(kf, 2)
    advance(vf)
    advance(kf, 2)
    scores(0, 0, NP)
    advance(vf)
    values(0, 0, NP)
    advance(vf)
    scores(1, 0, NP)
    advance(vf)
    values(1, 0, NP)
    vr = reduce(1, vo_ref)
    advance(vr)
    advance(vf)
    products(0, 0, NP)
    advance(vr)
    grads(0, 0, NP)
    products(1, 0, NP)
    grads(1, 0, NP)
    kr = reduce(0, ko_ref)
    advance(kr)
    queries(0, 0, NP)
    advance(vr)
    advance(kr)
    advance(vr)
    queries(1, 0, NP)
    leave = pltpu.make_async_copy(dq_ref, dq_hbm, s_in.at[9])
    leave.start()
    advance(vr)
    advance(kr, 2)
    advance(vr)
    for _ in kr:
        pass
    for _ in vr:
        pass
    leave.wait()
    for cp in sends:
        cp.wait_send()


def finish_kernel(a, b, c, ao, bo, co):
    ao[...] = a[...]
    bo[...] = b[...]
    co[...] = c[...]


def finish(*outs):
    return pl.pallas_call(finish_kernel, out_shape=tuple(jax.ShapeDtypeStruct(o.shape, o.dtype) for o in outs))(*outs)


def fused(lists, counts, span, row, k, v, q, do):
    vm = pl.BlockSpec(memory_space=pltpu.VMEM)
    hb = pl.BlockSpec(memory_space=pl.ANY)
    V = pltpu.VMEM
    D = pltpu.SemaphoreType.DMA
    tok = jax.ShapeDtypeStruct((32, NK * H), bf)
    return pl.pallas_call(
        kernel,
        out_shape=(jax.ShapeDtypeStruct((2 * B, R), bf), tok, tok),
        in_specs=[hb] * 8,
        out_specs=[hb, vm, vm],
        scratch_shapes=[
            V((NB, NBLK), jnp.int32), pltpu.SMEM((NBLK,), jnp.int32), pltpu.SMEM((NBLK,), jnp.int32), V((1, NBLK), jnp.int32),
            V((NB + 8, H), jnp.int32), pltpu.SMEM((NB + 8, H), jnp.int32),
            V((32, NK * H), bf), V((32, NK * H), bf), V((2 * B, R), bf), V((2 * B, R), bf), V((2 * B, R), bf),
            V((NK, 2, 32, H), bf), V((NBLK, B, H), bf), V((NBLK, B, H), bf), V((2, 2, 4, 4, 2, B, H), bf),
            V((2, H, R), bf), V((2, H, R), bf), V((2, R, H), bf), V((2, R, H), bf),
            V((2, NP, 2 * B, R), f32), V((NP, 2 * B, R), f32), V((2 * NB + 1, B, H), f32), V((H, R), f32),
            V((2, 8, R), f32), V((2, 8, R), f32), V((2, 8, R), f32),
            V((2, 4, 4, 2, B, H), bf), V((2, 4, 4, 2, B, H), bf), V((2, 3, 4, 2, B, H), bf),
            V((2, 3, 2, B, H), bf), V((2, 2, B, H), f32), V((2, NK, 32, H), bf), V((2, NK, 32, H), bf),
            D((10,)), D((2, 7)), D((2, 7)), D((2, 3)), D((2, 3)), D((2, 2, 4)), D((2, 2, 4)), D((2, 2, 4)), D((2, 2, 4)), D((2, 16)), D((2, 16)),
            D((2, 4)), D((2, 4)), D((2, 3, 4)), D((2, 3, 4)), D((2, 3)), D((2, 3)), D((2, 7)), D((2, 7)),
        ],
        compiler_params=pltpu.CompilerParams(collective_id=0, has_side_effects=True, vmem_limit_bytes=62 << 20),
    )(lists, counts, span, row, k, v, q, do)


def shards(queries, key_vector_rows, value_vector_rows, output_gradient, key_lists, block_counts, span_table):
    return finish(*fused(key_lists.T, block_counts, span_table, span_table.reshape(1, NBLK), key_vector_rows, value_vector_rows, queries, output_gradient))


def solution(mesh):
    tokens = P(("seq", "kvh"), None)
    heads = P("seq", "kvh")
    return jax.shard_map(
        shards,
        mesh=mesh,
        in_specs=(heads, tokens, tokens, heads, P(), P(), P()),
        out_specs=(heads, tokens, tokens),
        check_vma=False,
    )
```
